32 devices in a mesh: box: 8 (over z, x), path: 4 (over y, core).
Axes of the slice: x: 2, y: 2, z: 4, core: 2. Of those that a mesh axis runs over, the one named last changes fastest.
Arguments:
- features: float32 [1024, 9, 128], P('box'), may hold values from -6 to 6
- positions: float32 [3, 1024], P(None, 'box'), may hold values from 0 to 96, as said below
- cotangent: bfloat16 [1024, 9, 128], P('box'), may hold values from -6 to 6
- weights: float32 [8, 8, 128], P('path'), may hold values from -2 to 2
- neighbours: int32 [16, 3], P('box'), may hold values from 0 to 3, as said below
- send_list: int32 [8, 2], P('box'), may hold values from 0 to 1, as said below
Outputs:
- grad_features: float32 [1024, 9, 128], P(('box', 'path'))
- grad_weights: float32 [8, 8, 128], P('path')
The draws below stay inside these ranges and needn't reach their ends.
Inputs may be any that keep to these rules, and one draw needn't show every extreme that they name: `positions`: stored block s of box b has a place g = b * 2 + (a permutation of 0 to 1 within the box) along a chain; its atoms lie near the points of a grid of spacing 1.5 with 4 x 4 points across and 4 along the third coordinate, the first coordinate between 6 g and 6 g + 6, each moved by at most 0.35 in each coordinate. Blocks whose places differ by two or more have no atoms within 5 of each other. `neighbours`: row g lists the block itself (its stored index), the block one place before it and the block one place after it along the chain, as table indices: below 2 the box's own stored blocks, 2 the block received from the previous box (its last block along the chain), 3 the block received from the next box (its first block along the chain). The relation is symmetric. send_list[b, 0] is the stored index of the first block of box b's stretch of the chain and send_list[b, 1] that of the last.
All inputs are finite; a program needn't handle non-finite values.
Results may differ from the reference program's by a relative error of at most 0.0045.
Values may be sent and summed in bfloat16 or wider, within the bound.
A program may use at most 64 MiB of HBM per device.

```python
import math
import jax
import jax.numpy as jnp
from jax import lax

CHANNELS = 128
BASIS = 8
BLOCK = 64
NEIGHBOURS = 3
PATHS = 8
BLK_DEV = 2
BOXES = 8
BLOCKS = 16
ATOMS = 1024


def layout(key):
    keys = jax.random.split(jax.random.fold_in(key, 7), BOXES)

    def shuffle(subkey):
        return jax.random.permutation(subkey, BLK_DEV)
    orders = jax.vmap(shuffle)(keys).astype(jnp.int32)
    places = jnp.argsort(orders, axis=1, stable=True).astype(jnp.int32)
    return (orders, places)


def draw_positions(key, part):
    orders, places = layout(key)
    chain = (jnp.arange(BOXES, dtype=jnp.int32)[:, None] * BLK_DEV + orders).reshape(BLOCKS)
    atom = jnp.arange(BLOCK, dtype=jnp.int32)
    column_x = (atom % 4).astype(jnp.float32)
    column_y = (atom // 4 % 4).astype(jnp.float32)
    column_z = (atom // 16).astype(jnp.float32)
    spread = 0.3
    jitter = jax.random.uniform(jax.random.fold_in(key, 11), (3, BLOCKS, BLOCK), jnp.float32, -spread, spread)
    coord_x = 1.5 * (4.0 * chain[:, None].astype(jnp.float32) + column_x[None] + 0.5)
    coord_y = jnp.broadcast_to(1.5 * (column_y[None] + 0.5), (BLOCKS, BLOCK))
    coord_z = jnp.broadcast_to(1.5 * (column_z[None] + 0.5), (BLOCKS, BLOCK))
    grid = jnp.stack([coord_x, coord_y, coord_z]) + jitter
    return grid.reshape(3, ATOMS).astype(jnp.float32)


def draw_neighbours(key, part):
    orders, places = layout(key)
    earlier = orders - 1
    later = orders + 1
    earlier_slot = jnp.take_along_axis(places, jnp.clip(earlier, 0, BLK_DEV - 1), axis=1)
    later_slot = jnp.take_along_axis(places, jnp.clip(later, 0, BLK_DEV - 1), axis=1)
    earlier_slot = jnp.where(earlier < 0, BLK_DEV, earlier_slot)
    later_slot = jnp.where(later > BLK_DEV - 1, BLK_DEV + 1, later_slot)
    itself = jnp.broadcast_to(jnp.arange(BLK_DEV, dtype=jnp.int32)[None], (BOXES, BLK_DEV))
    listing = jnp.stack([itself, earlier_slot, later_slot], axis=2)
    return listing.reshape(BLOCKS, 3).astype(jnp.int32)


def draw_send_list(key, part):
    orders, places = layout(key)
    return jnp.stack([places[:, 0], places[:, BLK_DEV - 1]], axis=1).astype(jnp.int32)


def block_levels(own_key, shape, cuts, smallest, largest):
    level, own = 1.0, jax.random.fold_in(own_key, 6)
    for axis_at, blocks in cuts:
        heights = jnp.exp(jax.random.uniform(jax.random.fold_in(own, axis_at), (blocks,), jnp.float32, smallest / len(cuts), largest / len(cuts)))
        level = level * jnp.repeat(heights, shape[axis_at] // blocks).reshape([-1 if axis == axis_at else 1 for axis in range(len(shape))])
    return level


def normal_values(stream_key, dims, width, reach, cuts=(), kind=jnp.bfloat16):
    entries = width * jax.random.normal(stream_key, dims, jnp.float32)
    if cuts:
        entries = entries * block_levels(stream_key, dims, cuts, -0.22, 0.18)
    return jnp.clip(entries, -reach, reach).astype(kind)


def setup_inputs(seed: int = 0) -> dict:
    arg_keys = jax.random.split(jax.random.key(seed), 7)
    return {
        "features": normal_values(arg_keys[0], (ATOMS, 9, CHANNELS), 1.0, 6.0, ((0, 8),), jnp.float32),
        "positions": draw_positions(jax.random.fold_in(arg_keys[6], 71), 0),
        "cotangent": normal_values(arg_keys[2], (ATOMS, 9, CHANNELS), 1.0, 6.0, ((0, 8),)),
        "weights": normal_values(arg_keys[3], (PATHS, BASIS, CHANNELS), BASIS ** -0.5, 2.0, ((0, 4),), jnp.float32),
        "neighbours": draw_neighbours(jax.random.fold_in(arg_keys[6], 71), 0),
        "send_list": draw_send_list(jax.random.fold_in(arg_keys[6], 71), 0),
    }


cutoff_radius = 5.0
edge_scale = 0.2
basis_width = 0.8
root_three = math.sqrt(3.0)
path_terms = [[(0, [(0, 0, 1.0)])], [(0, [(1, 1, 1.0), (2, 2, 1.0), (3, 3, 1.0)])], [(1, [(1, 0, 1.0)]), (2, [(2, 0, 1.0)]), (3, [(3, 0, 1.0)])], [(1, [(0, 1, 1.0)]), (2, [(0, 2, 1.0)]), (3, [(0, 3, 1.0)])], [(4, [(4, 0, 1.0)]), (5, [(5, 0, 1.0)]), (6, [(6, 0, 1.0)]), (7, [(7, 0, 1.0)]), (8, [(8, 0, 1.0)])], [(4, [(0, 4, 1.0)]), (5, [(0, 5, 1.0)]), (6, [(0, 6, 1.0)]), (7, [(0, 7, 1.0)]), (8, [(0, 8, 1.0)])], [(1, [(3, 2, 1.0), (2, 3, -1.0)]), (2, [(1, 3, 1.0), (3, 1, -1.0)]), (3, [(2, 1, 1.0), (1, 2, -1.0)])], [(0, [(4, 4, 1.0), (5, 5, 1.0), (6, 6, 1.0), (7, 7, 1.0), (8, 8, 1.0)])]]

def edge_tensor(anchor, target):
    offset = target[:, None, :] - anchor[:, :, None]
    square = lax.optimization_barrier(jnp.sum(offset * offset, axis=0))
    inside = square > 0.01
    distance = jnp.sqrt(jnp.where(inside, square, 1.0))
    direction = offset / distance[None]
    envelope = jnp.where(inside & (distance < cutoff_radius), 0.5 * (jnp.cos(math.pi * distance / cutoff_radius) + 1.0), 0.0)
    centres = (jnp.arange(BASIS, dtype=jnp.float32) + 0.5) * (cutoff_radius / BASIS)
    radial = jnp.exp(-jnp.square((distance[None] - centres[:, None, None]) / basis_width)) * (edge_scale * envelope)[None]
    eastward = direction[0]
    northward = direction[1]
    upward = direction[2]
    harmonics = jnp.stack([jnp.ones_like(eastward), eastward, northward, upward, root_three * eastward * northward, root_three * northward * upward, 0.5 * (3.0 * upward * upward - 1.0), root_three * eastward * upward, 0.5 * root_three * (eastward * eastward - northward * northward)])
    return (harmonics[:, None] * radial[None]).astype(jnp.bfloat16)

def forward_terms(paths, weights, edge_table, rounded):
    rows = rounded.shape[0]
    channels = rounded.shape[2]
    outputs = [jnp.zeros((rows, channels), jnp.float32) for output in range(9)]
    for weight_slot, path_number in enumerate(paths):
        for output, term_list in path_terms[path_number]:
            pieces = []
            stacked = []
            for harmonic, source, factor in term_list:
                signed = edge_table[harmonic] if factor > 0 else -edge_table[harmonic]
                pieces.append(signed.reshape(BASIS * rows, rows))
                stacked.append(rounded[:, source, :])
            product = jnp.dot(jnp.concatenate(pieces, axis=1), jnp.concatenate(stacked, axis=0), preferred_element_type=jnp.float32)
            product = product.reshape(BASIS, rows, channels)
            outputs[output] = outputs[output] + lax.optimization_barrier(jnp.sum(weights[weight_slot][:, None, :] * product, axis=0))
    return jnp.stack(outputs, axis=1)

def transpose_terms(paths, weights, edge_table, cotangent_rows, source_features):
    rows = source_features.shape[0]
    channels = source_features.shape[2]
    outputs = [jnp.zeros((rows, channels), jnp.float32) for output in range(9)]
    weight_parts = []
    for weight_slot, path_number in enumerate(paths):
        weight_part = jnp.zeros((BASIS, channels), jnp.float32)
        for output, term_list in path_terms[path_number]:
            for harmonic, source, factor in term_list:
                gathered = lax.dot_general(edge_table[harmonic].astype(jnp.float32), cotangent_rows[:, output, :].astype(jnp.float32), (((1,), (0,)), ((), ())), precision=lax.Precision.HIGHEST, preferred_element_type=jnp.float32)
                outputs[source] = outputs[source] + factor * lax.optimization_barrier(jnp.sum(weights[weight_slot][:, None, :] * gathered, axis=0))
                weight_part = weight_part + factor * lax.optimization_barrier(jnp.sum(source_features[:, source, :][None] * gathered, axis=1))
        weight_parts.append(weight_part)
    return (jnp.stack(outputs, axis=1), jnp.stack(weight_parts, axis=0))

def gate_back(message, cotangent):
    incoming = cotangent.astype(jnp.float32)
    scalar = message[:, 0]
    sigma = jax.nn.sigmoid(scalar)
    slope = sigma * (1.0 + scalar * (1.0 - sigma))
    coupling = lax.optimization_barrier(jnp.sum(incoming[:, 1:] * message[:, 1:], axis=1))
    leading = incoming[:, 0] * slope + sigma * (1.0 - sigma) * coupling
    others = incoming[:, 1:] * sigma[:, None]
    return jnp.concatenate([leading[:, None], others], axis=1).astype(jnp.bfloat16)

def reference(features, positions, cotangent, weights, neighbours, send_list):
    total_blocks = neighbours.shape[0]
    boxes = send_list.shape[0]
    per_box = total_blocks // boxes
    channels = features.shape[2]
    block_features = features.reshape(total_blocks, BLOCK, 9, channels)
    block_rounded = block_features.astype(jnp.bfloat16)
    block_places = positions.reshape(3, total_blocks, BLOCK).transpose(1, 0, 2)
    owner = (jnp.arange(total_blocks, dtype=jnp.int32) // per_box)[:, None]
    before = jnp.maximum(owner - 1, 0)
    after = jnp.minimum(owner + 1, boxes - 1)
    from_before = before * per_box + send_list[before[:, 0], 1][:, None]
    from_after = after * per_box + send_list[after[:, 0], 0][:, None]
    sources = jnp.where(neighbours < per_box, owner * per_box + neighbours, jnp.where(neighbours == per_box, from_before, from_after)).astype(jnp.int32)
    present = (neighbours < per_box) | (neighbours == per_box) & (owner > 0) | (neighbours == per_box + 1) & (owner < boxes - 1)
    present_weight = present.astype(jnp.float32)
    all_paths = list(range(PATHS))

    def forward_block(number):
        total = jnp.zeros((BLOCK, 9, channels), jnp.float32)
        for neighbour in range(NEIGHBOURS):
            source_block = sources[number, neighbour]
            edge_table = edge_tensor(block_places[number], block_places[source_block])
            rounded = block_rounded[source_block] * present[number, neighbour].astype(jnp.bfloat16)
            total = total + forward_terms(all_paths, weights, edge_table, rounded)
        return total
    message = lax.map(forward_block, jnp.arange(total_blocks, dtype=jnp.int32))
    message_cotangent = gate_back(message.reshape(-1, 9, channels), cotangent).reshape(total_blocks, BLOCK, 9, channels)

    def backward_block(carry, number):
        gradient, weight_total = carry
        for neighbour in range(NEIGHBOURS):
            source_block = sources[number, neighbour]
            scaling = present_weight[number, neighbour]
            edge_table = edge_tensor(block_places[number], block_places[source_block])
            contribution, weight_part = transpose_terms(all_paths, weights, edge_table, message_cotangent[number], block_features[source_block])
            gradient = gradient.at[source_block].add(scaling * contribution)
            weight_total = weight_total + scaling * weight_part
        return ((gradient, weight_total), None)
    starting = (jnp.zeros((total_blocks, BLOCK, 9, channels), jnp.float32), jnp.zeros((PATHS, BASIS, channels), jnp.float32))
    (gradient, weight_total), unused = lax.scan(backward_block, starting, jnp.arange(total_blocks, dtype=jnp.int32))
    grad_features = gradient.reshape(-1, 9, channels) + cotangent.astype(jnp.float32)
    return (grad_features, weight_total / math.sqrt(features.shape[0]))
```

```python
import functools
import math

import jax
import jax.numpy as jnp
from jax import lax
from jax.experimental import pallas as pl
from jax.experimental.pallas import tpu as pltpu
from jax.sharding import PartitionSpec as P

BASIS = 8
BLOCK = 64
PATHS = 8
SLOTS = 4

cutoff_radius = 5.0
edge_scale = 0.2
basis_width = 0.8
root_three = math.sqrt(3.0)
MESH = pl.DeviceIdType.MESH

GROUPS = ((0, 1, 2, 3), (0, 4, 5, 6), (0, 7, 8, None))
TILES = tuple((g, s) for g in range(3) for s in range(4) if GROUPS[g][s] is not None)
CROSS = {(1, 3): 1.0, (1, 2): -1.0, (2, 1): 1.0, (2, 3): -1.0, (3, 2): 1.0, (3, 1): -1.0}


def entry(g, s, slot):
    if GROUPS[g][slot] is None:
        return None
    if g == 0:
        if s == 0:
            return (0, 1.0) if slot == 0 else (3, 1.0)
        if slot == 0:
            return (2, 1.0)
        if slot == s:
            return (1, 1.0)
        return (6, CROSS[(s, slot)])
    if s == 0:
        return None if slot == 0 else (5, 1.0)
    if slot == 0:
        return (4, 1.0)
    return (7, 1.0) if slot == s else None


def parity(g, s):
    return -1.0 if g == 0 and s > 0 else 1.0


def kernel(
    boxes, ways, feat_ref, cot_ref, pos_ref, weight_ref, send_ref, grad_ref, gw_ref,
    edges, feats, cots, table, gates, halo_out, gate_out, place_out, place_in, all_weights,
    grad_out, grad_in, part_out, part_in,
    place_send, place_recv, halo_send, halo_recv, gate_send, gate_recv,
    weight_send, weight_recv, grad_send, grad_recv, part_send, part_recv,
):
    box = lax.axis_index("box")
    way = lax.axis_index("path")
    count = boxes * ways
    me = box * ways + way
    rows = feat_ref.shape[1]
    lanes = feat_ref.shape[2]
    width = lanes // ways
    share = rows // ways
    group_paths = PATHS // ways

    barrier = pltpu.get_barrier_semaphore()

    def greet(step, carry):
        other = lax.rem(me + step, count)
        pl.semaphore_signal(
            barrier, inc=1, device_id={"box": other // ways, "path": lax.rem(other, ways)},
            device_id_type=MESH,
        )
        return carry

    lax.fori_loop(1, count, greet, 0)

    slot_of = lax.broadcasted_iota(jnp.int32, (1, lanes), 1) // width
    first, last = box == 0, box == boxes - 1

    @pl.when(first)
    def _():
        place_in[0] = jnp.zeros_like(place_in[0])
        table[:, rows : rows + BLOCK] = jnp.zeros((3, BLOCK, lanes), table.dtype)
        gates[:, rows : rows + BLOCK] = jnp.zeros((3, BLOCK, lanes), gates.dtype)

    @pl.when(last)
    def _():
        place_in[1] = jnp.zeros_like(place_in[1])
        table[:, rows + BLOCK :] = jnp.zeros((3, BLOCK, lanes), table.dtype)
        gates[:, rows + BLOCK :] = jnp.zeros((3, BLOCK, lanes), gates.dtype)

    head, tail = send_ref[0, 0], send_ref[0, 1]
    places = pos_ref[...]
    turned = pltpu.roll(places, BLOCK, axis=1)
    place_out[0, 0:3] = jnp.where(tail == 0, places, turned)
    place_out[1, 0:3] = jnp.where(head == 1, places, turned)

    def packed(read, g):
        total = None
        for slot in range(SLOTS):
            component = GROUPS[g][slot]
            if component is None:
                continue
            shift = lax.rem((slot - way + ways) * width, lanes)
            moved = pltpu.roll(read(component), shift, axis=1)
            moved = jnp.where(slot_of == slot, moved, 0.0)
            total = moved if total is None else total + moved
        return total

    def pick(chosen, tile):
        return jnp.where(chosen == 0, tile[:BLOCK], tile[BLOCK:])

    for g in range(3):
        tile = packed(lambda q: feat_ref[q], g)
        feats[g] = tile
        table[g, 0:rows] = tile.astype(table.dtype)
        halo_out[0, g] = pick(tail, tile).astype(halo_out.dtype)
        halo_out[1, g] = pick(head, tile).astype(halo_out.dtype)
        cots[g] = packed(lambda q: cot_ref[q].astype(jnp.float32), g)

    pl.semaphore_wait(barrier, count - 1)

    def towards(side, source, target, send, recv):
        return pltpu.make_async_remote_copy(
            src_ref=source.at[side], dst_ref=target, send_sem=send.at[side],
            recv_sem=recv.at[side], device_id={"box": box + 1 - 2 * side, "path": way},
            device_id_type=MESH,
        )

    def halo_of(buffer, side):
        return buffer.at[:, pl.ds(rows + side * BLOCK, BLOCK), :]

    def place_copy(side):
        return towards(side, place_out, place_in.at[side], place_send, place_recv)

    def halo_copy(side):
        return towards(side, halo_out, halo_of(table, side), halo_send, halo_recv)

    def gate_copy(side):
        return towards(side, gate_out, halo_of(gates, side), gate_send, gate_recv)

    def if_sends(side, action):
        pl.when(box < boxes - 1 if side == 0 else box > 0)(action)

    def if_receives(side, action):
        pl.when(box > 0 if side == 0 else box < boxes - 1)(action)

    for side in range(2):
        if_sends(side, lambda side=side: place_copy(side).start())
    for side in range(2):
        if_sends(side, lambda side=side: halo_copy(side).start())

    def weight_copy(step):
        return pltpu.make_async_remote_copy(
            src_ref=weight_ref, dst_ref=all_weights.at[step], send_sem=weight_send.at[step],
            recv_sem=weight_recv.at[step],
            device_id={"box": box, "path": lax.rem(way + step, ways)}, device_id_type=MESH,
        )

    for step in range(1, ways):
        weight_copy(step).start()

    across = [jnp.broadcast_to(places[c : c + 1], (rows, lanes)).T for c in range(3)]

    def edge_half(targets, column):
        chunk = 16
        for start in range(0, rows, chunk):
            offset = [targets[c] - across[c][start : start + chunk] for c in range(3)]
            square = offset[0] * offset[0] + offset[1] * offset[1] + offset[2] * offset[2]
            inside = square > 0.01
            safe = jnp.where(inside, square, 1.0)
            inverse = lax.rsqrt(safe)
            distance = safe * inverse
            east, north, up = [part * inverse for part in offset]
            half = jnp.minimum(distance, cutoff_radius) * (0.5 * math.pi / cutoff_radius)
            z = half * half
            cosine = 1.0 / 479001600.0
            for factor in (3628800.0, 40320.0, 720.0, 24.0, 2.0):
                sign = -1.0 if factor in (3628800.0, 720.0, 2.0) else 1.0
                cosine = cosine * z + sign / factor
            cosine = cosine * z + 1.0
            envelope = jnp.where(
                inside & (distance < cutoff_radius), edge_scale * (cosine * cosine), 0.0
            )
            harmonics = [
                None, east, north, up,
                root_three * east * north,
                root_three * north * up,
                0.5 * (3.0 * up * up - 1.0),
                root_three * east * up,
                0.5 * root_three * (east * east - north * north),
            ]
            for k in range(BASIS):
                centre = (k + 0.5) * (cutoff_radius / BASIS)
                scaled = (distance - centre) * (1.0 / basis_width)
                radial = jnp.exp(-(scaled * scaled)) * envelope
                for y in range(9):
                    value = radial if y == 0 else harmonics[y] * radial
                    edges[
                        y, k * rows + start : k * rows + start + chunk, column : column + lanes
                    ] = value.astype(edges.dtype)

    edge_half([places[c : c + 1] for c in range(3)], 0)

    for side in range(2):
        if_receives(side, lambda side=side: place_copy(side).wait_recv())
    left = lax.broadcasted_iota(jnp.int32, (1, lanes), 1) < BLOCK
    beside = jnp.where(left, place_in[0, 0:3], place_in[1, 0:3])
    edge_half([beside[c : c + 1] for c in range(3)], lanes)

    for step in range(1, ways):
        weight_copy(step).wait_recv()

    def fold(tile):
        tile = tile + pltpu.roll(tile, width, axis=tile.ndim - 1)
        return tile + pltpu.roll(tile, 2 * width, axis=tile.ndim - 1)

    mine = slot_of == way
    by_step = []
    for step in range(ways):
        held = weight_ref if step == 0 else all_weights.at[step]
        by_step.append([fold(jnp.where(mine, held[n], 0.0)) for n in range(group_paths)])
    spread = []
    for path_number in range(PATHS):
        owner, n = divmod(path_number, group_paths)
        value = by_step[0][n]
        for step in range(1, ways):
            value = jnp.where(lax.rem(way - step + ways, ways) == owner, by_step[step][n], value)
        spread.append(value)

    def tile_weights(g, s, back):
        total = jnp.zeros((BASIS, lanes), jnp.float32)
        for slot in range(SLOTS):
            found = entry(g, s, slot if back else slot ^ s)
            if found is None:
                continue
            sign = found[1] * (parity(g, s) if back else 1.0)
            total = jnp.where(slot_of == slot, sign * spread[found[0]], total)
        return total

    lane_in = lax.broadcasted_iota(jnp.int32, (lanes, lanes), 0)
    lane_out = lax.broadcasted_iota(jnp.int32, (lanes, lanes), 1)
    same_channel = lane_in % width == lane_out % width

    def exchanged(tile, s):
        if s == 0:
            return tile
        matrix = same_channel & ((lane_in // width) == ((lane_out // width) ^ s))
        return jnp.dot(
            tile, matrix.astype(jnp.float32).astype(jnp.bfloat16),
            preferred_element_type=jnp.float32,
        ).astype(jnp.bfloat16)

    def product(source, g, s):
        y = 0 if s == 0 else GROUPS[g][s]
        return jnp.dot(
            edges[y], exchanged(source[g], s), preferred_element_type=jnp.float32
        )

    for side in range(2):
        if_receives(side, lambda side=side: halo_copy(side).wait_recv())

    message = [jnp.zeros((rows, lanes), jnp.float32) for g in range(3)]
    for g, s in TILES:
        value = product(table, g, s)
        weights = tile_weights(g, s, False)
        for k in range(BASIS):
            message[g] = message[g] + weights[k : k + 1] * value[k * rows : (k + 1) * rows]

    leading = slot_of == 0
    scalar = fold(jnp.where(leading, message[0] + message[1] + message[2], 0.0))
    sigma = jax.nn.sigmoid(scalar)
    incoming = [cots[g] for g in range(3)]
    coupled = incoming[0] * message[0] + incoming[1] * message[1] + incoming[2] * message[2]
    coupling = fold(jnp.where(leading, 0.0, coupled))
    slope = sigma * (1.0 + scalar * (1.0 - sigma))
    damped = sigma * (1.0 - sigma) * coupling
    for g in range(3):
        gate = jnp.where(leading, incoming[g] * slope + damped, sigma * incoming[g])
        gates[g, 0:rows] = gate.astype(gates.dtype)
        gate_out[0, g] = pick(tail, gate).astype(gate_out.dtype)
        gate_out[1, g] = pick(head, gate).astype(gate_out.dtype)
    for side in range(2):
        if_sends(side, lambda side=side: gate_copy(side).start())
    for side in range(2):
        if_receives(side, lambda side=side: gate_copy(side).wait_recv())

    gradient = [jnp.zeros((rows, lanes), jnp.float32) for g in range(3)]
    parts = [jnp.zeros((BASIS, lanes), jnp.float32) for path_number in range(PATHS)]
    for g, s in TILES:
        value = product(gates, g, s)
        weights = tile_weights(g, s, True)
        source = feats[g]
        sums = []
        for k in range(BASIS):
            piece = value[k * rows : (k + 1) * rows]
            gradient[g] = gradient[g] + weights[k : k + 1] * piece
            sums.append(jnp.sum(source * piece, axis=0, keepdims=True))
        summed = jnp.concatenate(sums, axis=0)
        for slot in range(SLOTS):
            found = entry(g, s, slot)
            if found is None:
                continue
            sign = found[1] * parity(g, s)
            parts[found[0]] = parts[found[0]] + jnp.where(slot_of == slot, sign * summed, 0.0)

    totals = [fold(part) for part in parts]
    for t in range(ways):
        tile = jnp.zeros((BASIS, lanes), jnp.float32)
        for n in range(group_paths):
            tile = jnp.where(slot_of == n, totals[t * group_paths + n], tile)
        part_out[t] = tile

    def part_send_step(step, carry):
        other = lax.rem(me + step, count)
        pltpu.make_async_remote_copy(
            src_ref=part_out.at[lax.rem(other, ways)], dst_ref=part_in.at[step - 1],
            send_sem=part_send, recv_sem=part_recv,
            device_id={"box": other // ways, "path": lax.rem(other, ways)}, device_id_type=MESH,
        ).start()
        return carry

    lax.fori_loop(1, count, part_send_step, 0)

    gradient[0] = gradient[0] + jnp.where(leading, gradient[1] + gradient[2], 0.0)
    for g in range(3):
        for t in range(ways):
            grad_out[t, g] = gradient[g][t * share : (t + 1) * share]

    def grad_copy(step):
        other = lax.rem(way + step, ways)
        return pltpu.make_async_remote_copy(
            src_ref=grad_out.at[other], dst_ref=grad_in.at[step - 1],
            send_sem=grad_send.at[step - 1], recv_sem=grad_recv.at[step - 1],
            device_id={"box": box, "path": other}, device_id_type=MESH,
        )

    for step in range(1, ways):
        grad_copy(step).start()
    for step in range(1, ways):
        grad_copy(step).wait_recv()
    for g in range(3):
        for slot in range(SLOTS):
            component = GROUPS[g][slot]
            if component is None or (g > 0 and slot == 0):
                continue
            total = None
            for step in range(ways):
                owner = lax.rem(way - step + ways, ways)
                held = grad_out[way, g] if step == 0 else grad_in[step - 1, g]
                shift = lax.rem((owner - slot + ways) * width, lanes)
                moved = jnp.where(slot_of == owner, pltpu.roll(held, shift, axis=1), 0.0)
                total = moved if total is None else total + moved
            grad_ref[component] = total

    whole = pltpu.make_async_copy(part_in, part_in, part_recv)
    whole.wait()
    collected = [part_out[way]] + [None] * (ways - 1)

    def collect(batch, carry):
        return tuple(carry[r] + part_in[batch * ways + r] for r in range(ways))

    empty = tuple(jnp.zeros((BASIS, lanes), jnp.float32) for r in range(ways))
    sums = list(lax.fori_loop(0, boxes - 1, collect, empty))
    for r in range(ways - 1):
        sums[r] = sums[r] + part_in[(boxes - 1) * ways + r]
    collected = [sums[ways - 1] + part_out[way]] + sums[: ways - 1]
    scale = 1.0 / math.sqrt(rows * boxes)
    for n in range(group_paths):
        total = None
        for step in range(ways):
            owner = lax.rem(way - step + ways, ways)
            shift = lax.rem((owner - n + ways) * width, lanes)
            moved = jnp.where(slot_of == owner, pltpu.roll(collected[step], shift, axis=1), 0.0)
            total = moved if total is None else total + moved
        gw_ref[n] = total * scale

    for side in range(2):
        if_sends(side, lambda side=side: place_copy(side).wait_send())
        if_sends(side, lambda side=side: halo_copy(side).wait_send())
        if_sends(side, lambda side=side: gate_copy(side).wait_send())
    for step in range(1, ways):
        weight_copy(step).wait_send()
        grad_copy(step).wait_send()
    pltpu.make_async_copy(part_in, part_in, part_send).wait()


def solution(mesh):
    boxes, ways = mesh.shape["box"], mesh.shape["path"]

    def on_device(features, positions, cotangent, weights, neighbours, send_list):
        rows, components, lanes = features.shape
        share = rows // ways
        reach = rows + 2 * BLOCK
        f32, bf16 = jnp.float32, jnp.bfloat16
        vmem = pl.BlockSpec(memory_space=pltpu.VMEM)
        dma = pltpu.SemaphoreType.DMA
        moved, gw = pl.pallas_call(
            functools.partial(kernel, boxes, ways),
            name="layer_back",
            out_shape=(
                jax.ShapeDtypeStruct((components, share, lanes), f32),
                jax.ShapeDtypeStruct((PATHS // ways, BASIS, lanes), f32),
            ),
            in_specs=[vmem, vmem, vmem, vmem, pl.BlockSpec(memory_space=pltpu.SMEM)],
            out_specs=(vmem, vmem),
            scratch_shapes=[
                pltpu.VMEM((components, BASIS * rows, reach), bf16),
                pltpu.VMEM((3, rows, lanes), f32),
                pltpu.VMEM((3, rows, lanes), f32),
                pltpu.VMEM((3, reach, lanes), bf16),
                pltpu.VMEM((3, reach, lanes), bf16),
                pltpu.VMEM((2, 3, BLOCK, lanes), bf16),
                pltpu.VMEM((2, 3, BLOCK, lanes), bf16),
                pltpu.VMEM((2, 8, lanes), f32),
                pltpu.VMEM((2, 8, lanes), f32),
                pltpu.VMEM((ways, PATHS // ways, BASIS, lanes), f32),
                pltpu.VMEM((ways, 3, share, lanes), f32),
                pltpu.VMEM((ways - 1, 3, share, lanes), f32),
                pltpu.VMEM((ways, BASIS, lanes), f32),
                pltpu.VMEM((boxes * ways - 1, BASIS, lanes), f32),
                dma((2,)), dma((2,)), dma((2,)), dma((2,)), dma((2,)), dma((2,)),
                dma((ways,)), dma((ways,)), dma((ways - 1,)), dma((ways - 1,)), dma, dma,
            ],
            compiler_params=pltpu.CompilerParams(collective_id=0, has_side_effects=True),
        )(
            features.transpose(1, 0, 2), cotangent.transpose(1, 0, 2), positions, weights,
            send_list,
        )
        own = lax.dynamic_slice_in_dim(cotangent, lax.axis_index("path") * share, share, 0)
        return moved.transpose(1, 0, 2) + own.astype(f32), gw

    placed = (
        P("box", None, None),
        P(None, "box"),
        P("box", None, None),
        P("path", None, None),
        P("box", None),
        P("box", None),
    )
    return jax.shard_map(
        on_device,
        mesh=mesh,
        in_specs=placed,
        out_specs=(P(("box", "path"), None, None), P("path", None, None)),
        check_vma=False,
    )
```

```python
import functools
import math

import jax
import jax.numpy as jnp
from jax import lax
from jax.experimental import pallas as pl
from jax.experimental.pallas import tpu as pltpu
from jax.sharding import PartitionSpec as P

BASIS = 8
BLOCK = 64
PATHS = 8
SLOTS = 4

cutoff_radius = 5.0
edge_scale = 0.2
basis_width = 0.8
root_three = math.sqrt(3.0)
MESH = pl.DeviceIdType.MESH

GROUPS = ((0, 1, 2, 3), (0, 4, 5, 6), (0, 7, 8, None))
TILES = tuple((g, s) for g in range(3) for s in range(4) if GROUPS[g][s] is not None)
CROSS = {(1, 3): 1.0, (1, 2): -1.0, (2, 1): 1.0, (2, 3): -1.0, (3, 2): 1.0, (3, 1): -1.0}


def entry(g, s, slot):
    if GROUPS[g][slot] is None:
        return None
    if g == 0:
        if s == 0:
            return (0, 1.0) if slot == 0 else (3, 1.0)
        if slot == 0:
            return (2, 1.0)
        if slot == s:
            return (1, 1.0)
        return (6, CROSS[(s, slot)])
    if s == 0:
        return None if slot == 0 else (5, 1.0)
    if slot == 0:
        return (4, 1.0)
    return (7, 1.0) if slot == s else None


def parity(g, s):
    return -1.0 if g == 0 and s > 0 else 1.0


def kernel(
    boxes, ways, feat_hbm, cot_hbm, pos_ref, weight_ref, send_ref, grad_ref, gw_ref,
    feat_ref, cot_ref, edges, feats, cots, table, gates, halo_out, gate_out, place_out, place_in, all_weights,
    grad_out, grad_in, part_out, part_in, grad_own,
    place_send, place_recv, halo_send, halo_recv, gate_send, gate_recv,
    weight_send, weight_recv, grad_send, grad_recv, part_send, part_recv, load_sem,
):
    box = lax.axis_index("box")
    way = lax.axis_index("path")
    count = boxes * ways
    me = box * ways + way
    rows = feat_ref.shape[1]
    lanes = feat_ref.shape[2]
    width = lanes // ways
    share = rows // ways
    group_paths = PATHS // ways

    feat_load = pltpu.make_async_copy(feat_hbm, feat_ref, load_sem.at[0])
    cot_load = pltpu.make_async_copy(cot_hbm, cot_ref, load_sem.at[1])
    feat_load.start()
    cot_load.start()
    barrier = pltpu.get_barrier_semaphore()

    def greet(step, carry):
        other = lax.rem(me + step, count)
        pl.semaphore_signal(
            barrier, inc=1, device_id={"box": other // ways, "path": lax.rem(other, ways)},
            device_id_type=MESH,
        )
        return carry

    lax.fori_loop(1, count, greet, 0)

    slot_of = lax.broadcasted_iota(jnp.int32, (1, lanes), 1) // width
    first, last = box == 0, box == boxes - 1

    @pl.when(first)
    def _():
        place_in[0] = jnp.zeros_like(place_in[0])
        table[:, rows : rows + BLOCK] = jnp.zeros((3, BLOCK, lanes), table.dtype)
        gates[:, rows : rows + BLOCK] = jnp.zeros((3, BLOCK, lanes), gates.dtype)

    @pl.when(last)
    def _():
        place_in[1] = jnp.zeros_like(place_in[1])
        table[:, rows + BLOCK :] = jnp.zeros((3, BLOCK, lanes), table.dtype)
        gates[:, rows + BLOCK :] = jnp.zeros((3, BLOCK, lanes), gates.dtype)

    head, tail = send_ref[0, 0], send_ref[0, 1]
    places = pos_ref[...]
    turned = pltpu.roll(places, BLOCK, axis=1)
    place_out[0, 0:3] = jnp.where(tail == 0, places, turned)
    place_out[1, 0:3] = jnp.where(head == 1, places, turned)

    def packed(read, g):
        total = None
        for slot in range(SLOTS):
            component = GROUPS[g][slot]
            if component is None:
                continue
            shift = lax.rem((slot - way + ways) * width, lanes)
            moved = pltpu.roll(read(component), shift, axis=1)
            moved = jnp.where(slot_of == slot, moved, 0.0)
            total = moved if total is None else total + moved
        return total

    def pick(chosen, tile):
        return jnp.where(chosen == 0, tile[:BLOCK], tile[BLOCK:])

    feat_load.wait()
    for g in range(3):
        tile = packed(lambda q: feat_ref[q], g)
        feats[g] = tile
        table[g, 0:rows] = tile.astype(table.dtype)
        halo_out[0, g] = pick(tail, tile).astype(halo_out.dtype)
        halo_out[1, g] = pick(head, tile).astype(halo_out.dtype)

    pl.semaphore_wait(barrier, count - 1)

    def towards(side, source, target, send, recv):
        return pltpu.make_async_remote_copy(
            src_ref=source.at[side], dst_ref=target, send_sem=send.at[side],
            recv_sem=recv.at[side], device_id={"box": box + 1 - 2 * side, "path": way},
            device_id_type=MESH,
        )

    def halo_of(buffer, side):
        return buffer.at[:, pl.ds(rows + side * BLOCK, BLOCK), :]

    def place_copy(side):
        return towards(side, place_out, place_in.at[side], place_send, place_recv)

    def halo_copy(side):
        return towards(side, halo_out, halo_of(table, side), halo_send, halo_recv)

    def gate_copy(side):
        return towards(side, gate_out, halo_of(gates, side), gate_send, gate_recv)

    def if_sends(side, action):
        pl.when(box < boxes - 1 if side == 0 else box > 0)(action)

    def if_receives(side, action):
        pl.when(box > 0 if side == 0 else box < boxes - 1)(action)

    for side in range(2):
        if_sends(side, lambda side=side: place_copy(side).start())
    for side in range(2):
        if_sends(side, lambda side=side: halo_copy(side).start())

    def weight_copy(step):
        return pltpu.make_async_remote_copy(
            src_ref=weight_ref, dst_ref=all_weights.at[step], send_sem=weight_send.at[step],
            recv_sem=weight_recv.at[step],
            device_id={"box": box, "path": lax.rem(way + step, ways)}, device_id_type=MESH,
        )

    for step in range(1, ways):
        weight_copy(step).start()

    cot_load.wait()
    for g in range(3):
        cots[g] = packed(lambda q: cot_ref[q].astype(jnp.float32), g)

    across = [jnp.broadcast_to(places[c : c + 1], (rows, lanes)).T for c in range(3)]

    def edge_half(targets, column):
        chunk = 16
        for start in range(0, rows, chunk):
            offset = [targets[c] - across[c][start : start + chunk] for c in range(3)]
            square = offset[0] * offset[0] + offset[1] * offset[1] + offset[2] * offset[2]
            inside = square > 0.01
            safe = jnp.where(inside, square, 1.0)
            inverse = lax.rsqrt(safe)
            distance = safe * inverse
            east, north, up = [part * inverse for part in offset]
            half = jnp.minimum(distance, cutoff_radius) * (0.5 * math.pi / cutoff_radius)
            z = half * half
            cosine = 1.0 / 479001600.0
            for factor in (3628800.0, 40320.0, 720.0, 24.0, 2.0):
                sign = -1.0 if factor in (3628800.0, 720.0, 2.0) else 1.0
                cosine = cosine * z + sign / factor
            cosine = cosine * z + 1.0
            envelope = jnp.where(
                inside & (distance < cutoff_radius), edge_scale * (cosine * cosine), 0.0
            )
            harmonics = [
                None, east, north, up,
                root_three * east * north,
                root_three * north * up,
                0.5 * (3.0 * up * up - 1.0),
                root_three * east * up,
                0.5 * root_three * (east * east - north * north),
            ]
            for k in range(BASIS):
                centre = (k + 0.5) * (cutoff_radius / BASIS)
                scaled = (distance - centre) * (1.0 / basis_width)
                radial = jnp.exp(-(scaled * scaled)) * envelope
                for y in range(9):
                    value = radial if y == 0 else harmonics[y] * radial
                    edges[
                        y, k * rows + start : k * rows + start + chunk, column : column + lanes
                    ] = value.astype(edges.dtype)

    edge_half([places[c : c + 1] for c in range(3)], 0)

    for side in range(2):
        if_receives(side, lambda side=side: place_copy(side).wait_recv())
    left = lax.broadcasted_iota(jnp.int32, (1, lanes), 1) < BLOCK
    beside = jnp.where(left, place_in[0, 0:3], place_in[1, 0:3])
    edge_half([beside[c : c + 1] for c in range(3)], lanes)

    for step in range(1, ways):
        weight_copy(step).wait_recv()

    def fold(tile):
        tile = tile + pltpu.roll(tile, width, axis=tile.ndim - 1)
        return tile + pltpu.roll(tile, 2 * width, axis=tile.ndim - 1)

    mine = slot_of == way
    by_step = []
    for step in range(ways):
        held = weight_ref if step == 0 else all_weights.at[step]
        by_step.append([fold(jnp.where(mine, held[n], 0.0)) for n in range(group_paths)])
    spread = []
    for path_number in range(PATHS):
        owner, n = divmod(path_number, group_paths)
        value = by_step[0][n]
        for step in range(1, ways):
            value = jnp.where(lax.rem(way - step + ways, ways) == owner, by_step[step][n], value)
        spread.append(value)

    def tile_weights(g, s, back):
        total = jnp.zeros((BASIS, lanes), jnp.float32)
        for slot in range(SLOTS):
            found = entry(g, s, slot if back else slot ^ s)
            if found is None:
                continue
            sign = found[1] * (parity(g, s) if back else 1.0)
            total = jnp.where(slot_of == slot, sign * spread[found[0]], total)
        return total

    lane_in = lax.broadcasted_iota(jnp.int32, (lanes, lanes), 0)
    lane_out = lax.broadcasted_iota(jnp.int32, (lanes, lanes), 1)
    same_channel = lane_in % width == lane_out % width

    def exchanged(tile, s):
        if s == 0:
            return tile
        matrix = same_channel & ((lane_in // width) == ((lane_out // width) ^ s))
        return jnp.dot(
            tile, matrix.astype(jnp.float32).astype(jnp.bfloat16),
            preferred_element_type=jnp.float32,
        ).astype(jnp.bfloat16)

    def product(source, g, s):
        y = 0 if s == 0 else GROUPS[g][s]
        return jnp.dot(
            edges[y], exchanged(source[g], s), preferred_element_type=jnp.float32
        )

    for side in range(2):
        if_receives(side, lambda side=side: halo_copy(side).wait_recv())

    message = [jnp.zeros((rows, lanes), jnp.float32) for g in range(3)]
    for g, s in TILES:
        value = product(table, g, s)
        weights = tile_weights(g, s, False)
        for k in range(BASIS):
            message[g] = message[g] + weights[k : k + 1] * value[k * rows : (k + 1) * rows]

    leading = slot_of == 0
    scalar = fold(jnp.where(leading, message[0] + message[1] + message[2], 0.0))
    sigma = jax.nn.sigmoid(scalar)
    incoming = [cots[g] for g in range(3)]
    coupled = incoming[0] * message[0] + incoming[1] * message[1] + incoming[2] * message[2]
    coupling = fold(jnp.where(leading, 0.0, coupled))
    slope = sigma * (1.0 + scalar * (1.0 - sigma))
    damped = sigma * (1.0 - sigma) * coupling
    for g in range(3):
        gate = jnp.where(leading, incoming[g] * slope + damped, sigma * incoming[g])
        gates[g, 0:rows] = gate.astype(gates.dtype)
        gate_out[0, g] = pick(tail, gate).astype(gate_out.dtype)
        gate_out[1, g] = pick(head, gate).astype(gate_out.dtype)
    for side in range(2):
        if_sends(side, lambda side=side: gate_copy(side).start())
    for side in range(2):
        if_receives(side, lambda side=side: gate_copy(side).wait_recv())

    gradient = [jnp.zeros((rows, lanes), jnp.float32) for g in range(3)]
    parts = [jnp.zeros((BASIS, lanes), jnp.float32) for path_number in range(PATHS)]
    for g, s in TILES:
        value = product(gates, g, s)
        weights = tile_weights(g, s, True)
        source = feats[g]
        sums = []
        for k in range(BASIS):
            piece = value[k * rows : (k + 1) * rows]
            gradient[g] = gradient[g] + weights[k : k + 1] * piece
            sums.append(jnp.sum(source * piece, axis=0, keepdims=True))
        summed = jnp.concatenate(sums, axis=0)
        for slot in range(SLOTS):
            found = entry(g, s, slot)
            if found is None:
                continue
            sign = found[1] * parity(g, s)
            parts[found[0]] = parts[found[0]] + jnp.where(slot_of == slot, sign * summed, 0.0)

    totals = [fold(part) for part in parts]
    for t in range(ways):
        tile = jnp.zeros((BASIS, lanes), jnp.float32)
        for n in range(group_paths):
            tile = jnp.where(slot_of == n, totals[t * group_paths + n], tile)
        part_out[t] = tile

    def part_send_step(step, carry):
        other = lax.rem(me + step, count)
        pltpu.make_async_remote_copy(
            src_ref=part_out.at[lax.rem(other, ways)], dst_ref=part_in.at[step - 1],
            send_sem=part_send, recv_sem=part_recv,
            device_id={"box": other // ways, "path": lax.rem(other, ways)}, device_id_type=MESH,
        ).start()
        return carry

    lax.fori_loop(1, count, part_send_step, 0)

    gradient[0] = gradient[0] + jnp.where(leading, gradient[1] + gradient[2], 0.0)
    for g in range(3):
        for t in range(ways):
            grad_out[t, g] = gradient[g][t * share : (t + 1) * share].astype(grad_out.dtype)
        grad_own[g] = gradient[g]

    def grad_copy(step):
        other = lax.rem(way + step, ways)
        return pltpu.make_async_remote_copy(
            src_ref=grad_out.at[other], dst_ref=grad_in.at[step - 1],
            send_sem=grad_send.at[step - 1], recv_sem=grad_recv.at[step - 1],
            device_id={"box": box, "path": other}, device_id_type=MESH,
        )

    for step in range(1, ways):
        grad_copy(step).start()
    own_rows = pl.ds(pl.multiple_of(way * share, share), share)
    for step in range(1, ways):
        grad_copy(step).wait_recv()
    for g in range(3):
        for slot in range(SLOTS):
            component = GROUPS[g][slot]
            if component is None or (g > 0 and slot == 0):
                continue
            total = None
            for step in range(ways):
                owner = lax.rem(way - step + ways, ways)
                held = grad_own[g, own_rows] if step == 0 else grad_in[step - 1, g]
                held = held.astype(jnp.float32)
                shift = lax.rem((owner - slot + ways) * width, lanes)
                moved = jnp.where(slot_of == owner, pltpu.roll(held, shift, axis=1), 0.0)
                total = moved if total is None else total + moved
            grad_ref[component] = total + cot_ref[component, own_rows].astype(jnp.float32)

    whole = pltpu.make_async_copy(part_in, part_in, part_recv)
    whole.wait()
    collected = [part_out[way]] + [None] * (ways - 1)

    def collect(batch, carry):
        return tuple(carry[r] + part_in[batch * ways + r] for r in range(ways))

    empty = tuple(jnp.zeros((BASIS, lanes), jnp.float32) for r in range(ways))
    sums = list(lax.fori_loop(0, boxes - 1, collect, empty))
    for r in range(ways - 1):
        sums[r] = sums[r] + part_in[(boxes - 1) * ways + r]
    collected = [sums[ways - 1] + part_out[way]] + sums[: ways - 1]
    scale = 1.0 / math.sqrt(rows * boxes)
    for n in range(group_paths):
        total = None
        for step in range(ways):
            owner = lax.rem(way - step + ways, ways)
            shift = lax.rem((owner - n + ways) * width, lanes)
            moved = jnp.where(slot_of == owner, pltpu.roll(collected[step], shift, axis=1), 0.0)
            total = moved if total is None else total + moved
        gw_ref[n] = total * scale

    for side in range(2):
        if_sends(side, lambda side=side: place_copy(side).wait_send())
        if_sends(side, lambda side=side: halo_copy(side).wait_send())
        if_sends(side, lambda side=side: gate_copy(side).wait_send())
    for step in range(1, ways):
        weight_copy(step).wait_send()
        grad_copy(step).wait_send()
    pltpu.make_async_copy(part_in, part_in, part_send).wait()


def solution(mesh):
    boxes, ways = mesh.shape["box"], mesh.shape["path"]

    def on_device(features, positions, cotangent, weights, neighbours, send_list):
        rows, components, lanes = features.shape
        share = rows // ways
        reach = rows + 2 * BLOCK
        f32, bf16 = jnp.float32, jnp.bfloat16
        vmem = pl.BlockSpec(memory_space=pltpu.VMEM)
        anywhere = pl.BlockSpec(memory_space=pl.ANY)
        dma = pltpu.SemaphoreType.DMA
        moved, gw = pl.pallas_call(
            functools.partial(kernel, boxes, ways),
            name="layer_back",
            out_shape=(
                jax.ShapeDtypeStruct((components, share, lanes), f32),
                jax.ShapeDtypeStruct((PATHS // ways, BASIS, lanes), f32),
            ),
            in_specs=[anywhere, anywhere, vmem, vmem, pl.BlockSpec(memory_space=pltpu.SMEM)],
            out_specs=(vmem, vmem),
            scratch_shapes=[
                pltpu.VMEM((components, rows, lanes), f32),
                pltpu.VMEM((components, rows, lanes), bf16),
                pltpu.VMEM((components, BASIS * rows, reach), bf16),
                pltpu.VMEM((3, rows, lanes), f32),
                pltpu.VMEM((3, rows, lanes), f32),
                pltpu.VMEM((3, reach, lanes), bf16),
                pltpu.VMEM((3, reach, lanes), bf16),
                pltpu.VMEM((2, 3, BLOCK, lanes), bf16),
                pltpu.VMEM((2, 3, BLOCK, lanes), bf16),
                pltpu.VMEM((2, 8, lanes), f32),
                pltpu.VMEM((2, 8, lanes), f32),
                pltpu.VMEM((ways, PATHS // ways, BASIS, lanes), f32),
                pltpu.VMEM((ways, 3, share, lanes), bf16),
                pltpu.VMEM((ways - 1, 3, share, lanes), bf16),
                pltpu.VMEM((ways, BASIS, lanes), f32),
                pltpu.VMEM((boxes * ways - 1, BASIS, lanes), f32),
                pltpu.VMEM((3, rows, lanes), f32),
                dma((2,)), dma((2,)), dma((2,)), dma((2,)), dma((2,)), dma((2,)),
                dma((ways,)), dma((ways,)), dma((ways - 1,)), dma((ways - 1,)), dma, dma,
                dma((2,)),
            ],
            compiler_params=pltpu.CompilerParams(collective_id=0, has_side_effects=True),
        )(
            features.transpose(1, 0, 2), cotangent.transpose(1, 0, 2), positions, weights,
            send_list,
        )
        return moved.transpose(1, 0, 2), gw

    placed = (
        P("box", None, None),
        P(None, "box"),
        P("box", None, None),
        P("path", None, None),
        P("box", None),
        P("box", None),
    )
    return jax.shard_map(
        on_device,
        mesh=mesh,
        in_specs=placed,
        out_specs=(P(("box", "path"), None, None), P("path", None, None)),
        check_vma=False,
    )
```

```python
import functools
import math

import jax
import jax.numpy as jnp
from jax import lax
from jax.experimental import pallas as pl
from jax.experimental.pallas import tpu as pltpu
from jax.sharding import PartitionSpec as P

BASIS = 8
BLOCK = 64
PATHS = 8
SLOTS = 4

cutoff_radius = 5.0
edge_scale = 0.2
basis_width = 0.8
root_three = math.sqrt(3.0)
MESH = pl.DeviceIdType.MESH

GROUPS = ((0, 1, 2, 3), (0, 4, 5, 6), (0, 7, 8, None))
TILES = tuple((g, s) for g in range(3) for s in range(4) if GROUPS[g][s] is not None)
CROSS = {(1, 3): 1.0, (1, 2): -1.0, (2, 1): 1.0, (2, 3): -1.0, (3, 2): 1.0, (3, 1): -1.0}


def entry(g, s, slot):
    if GROUPS[g][slot] is None:
        return None
    if g == 0:
        if s == 0:
            return (0, 1.0) if slot == 0 else (3, 1.0)
        if slot == 0:
            return (2, 1.0)
        if slot == s:
            return (1, 1.0)
        return (6, CROSS[(s, slot)])
    if s == 0:
        return None if slot == 0 else (5, 1.0)
    if slot == 0:
        return (4, 1.0)
    return (7, 1.0) if slot == s else None


def parity(g, s):
    return -1.0 if g == 0 and s > 0 else 1.0


def kernel(
    boxes, ways, feat_hbm, cot_hbm, pos_ref, weight_ref, send_ref, grad_ref, gw_ref,
    feat_ref, cot_ref, edges, feats, cots, table, gates, halo_out, gate_out, place_out, place_in, all_weights,
    grad_out, grad_in, part_out, part_in, grad_own,
    place_send, place_recv, halo_send, halo_recv, gate_send, gate_recv,
    weight_send, weight_recv, grad_send, grad_recv, part_send, part_recv, load_sem,
):
    box = lax.axis_index("box")
    way = lax.axis_index("path")
    count = boxes * ways
    me = box * ways + way
    rows = feat_ref.shape[1]
    lanes = feat_ref.shape[2]
    width = lanes // ways
    share = rows // ways
    group_paths = PATHS // ways

    feat_load = pltpu.make_async_copy(feat_hbm, feat_ref, load_sem.at[0])
    cot_load = pltpu.make_async_copy(cot_hbm, cot_ref, load_sem.at[1])
    feat_load.start()
    cot_load.start()
    barrier = pltpu.get_barrier_semaphore()

    def greet(step, carry):
        other = lax.rem(me + step, count)
        pl.semaphore_signal(
            barrier, inc=1, device_id={"box": other // ways, "path": lax.rem(other, ways)},
            device_id_type=MESH,
        )
        return carry

    lax.fori_loop(1, count, greet, 0)

    slot_of = lax.broadcasted_iota(jnp.int32, (1, lanes), 1) // width
    first, last = box == 0, box == boxes - 1

    @pl.when(first)
    def _():
        place_in[0] = jnp.zeros_like(place_in[0])
        table[:, rows : rows + BLOCK] = jnp.zeros((3, BLOCK, lanes), table.dtype)
        gates[:, rows : rows + BLOCK] = jnp.zeros((3, BLOCK, lanes), gates.dtype)

    @pl.when(last)
    def _():
        place_in[1] = jnp.zeros_like(place_in[1])
        table[:, rows + BLOCK :] = jnp.zeros((3, BLOCK, lanes), table.dtype)
        gates[:, rows + BLOCK :] = jnp.zeros((3, BLOCK, lanes), gates.dtype)

    head, tail = send_ref[0, 0], send_ref[0, 1]
    places = pos_ref[...]
    turned = pltpu.roll(places, BLOCK, axis=1)
    place_out[0, 0:3] = jnp.where(tail == 0, places, turned)
    place_out[1, 0:3] = jnp.where(head == 1, places, turned)

    def packed(read, g):
        total = None
        for slot in range(SLOTS):
            component = GROUPS[g][slot]
            if component is None:
                continue
            shift = lax.rem((slot - way + ways) * width, lanes)
            moved = pltpu.roll(read(component), shift, axis=1)
            moved = jnp.where(slot_of == slot, moved, 0.0)
            total = moved if total is None else total + moved
        return total

    def pick(chosen, tile):
        return jnp.where(chosen == 0, tile[:BLOCK], tile[BLOCK:])

    feat_load.wait()
    for g in range(3):
        tile = packed(lambda q: feat_ref[q], g)
        feats[g] = tile
        table[g, 0:rows] = tile.astype(table.dtype)
        halo_out[0, g] = pick(tail, tile).astype(halo_out.dtype)
        halo_out[1, g] = pick(head, tile).astype(halo_out.dtype)

    pl.semaphore_wait(barrier, count - 1)

    def towards(side, source, target, send, recv):
        return pltpu.make_async_remote_copy(
            src_ref=source.at[side], dst_ref=target, send_sem=send.at[side],
            recv_sem=recv.at[side], device_id={"box": box + 1 - 2 * side, "path": way},
            device_id_type=MESH,
        )

    def group_copy(side, g, source, target, send, recv):
        return pltpu.make_async_remote_copy(
            src_ref=source.at[side, g],
            dst_ref=target.at[g, pl.ds(rows + side * BLOCK, BLOCK), :],
            send_sem=send.at[side, g], recv_sem=recv.at[side, g],
            device_id={"box": box + 1 - 2 * side, "path": way}, device_id_type=MESH,
        )

    def place_copy(side):
        return towards(side, place_out, place_in.at[side], place_send, place_recv)

    def halo_copy(side, g):
        return group_copy(side, g, halo_out, table, halo_send, halo_recv)

    def gate_copy(side, g):
        return group_copy(side, g, gate_out, gates, gate_send, gate_recv)

    def if_sends(side, action):
        pl.when(box < boxes - 1 if side == 0 else box > 0)(action)

    def if_receives(side, action):
        pl.when(box > 0 if side == 0 else box < boxes - 1)(action)

    for side in range(2):
        if_sends(side, lambda side=side: place_copy(side).start())
    for g in range(3):
        for side in range(2):
            if_sends(side, lambda side=side, g=g: halo_copy(side, g).start())

    def weight_copy(step):
        return pltpu.make_async_remote_copy(
            src_ref=weight_ref, dst_ref=all_weights.at[step], send_sem=weight_send.at[step],
            recv_sem=weight_recv.at[step],
            device_id={"box": box, "path": lax.rem(way + step, ways)}, device_id_type=MESH,
        )

    for step in range(1, ways):
        weight_copy(step).start()

    cot_load.wait()
    for g in range(3):
        cots[g] = packed(lambda q: cot_ref[q].astype(jnp.float32), g)

    across = [jnp.broadcast_to(places[c : c + 1], (rows, lanes)).T for c in range(3)]

    def edge_half(targets, column):
        chunk = 16
        for start in range(0, rows, chunk):
            offset = [targets[c] - across[c][start : start + chunk] for c in range(3)]
            square = offset[0] * offset[0] + offset[1] * offset[1] + offset[2] * offset[2]
            inside = square > 0.01
            safe = jnp.where(inside, square, 1.0)
            inverse = lax.rsqrt(safe)
            distance = safe * inverse
            east, north, up = [part * inverse for part in offset]
            half = jnp.minimum(distance, cutoff_radius) * (0.5 * math.pi / cutoff_radius)
            z = half * half
            cosine = 1.0 / 479001600.0
            for factor in (3628800.0, 40320.0, 720.0, 24.0, 2.0):
                sign = -1.0 if factor in (3628800.0, 720.0, 2.0) else 1.0
                cosine = cosine * z + sign / factor
            cosine = cosine * z + 1.0
            envelope = jnp.where(
                inside & (distance < cutoff_radius), edge_scale * (cosine * cosine), 0.0
            )
            harmonics = [
                None, east, north, up,
                root_three * east * north,
                root_three * north * up,
                0.5 * (3.0 * up * up - 1.0),
                root_three * east * up,
                0.5 * root_three * (east * east - north * north),
            ]
            for k in range(BASIS):
                centre = (k + 0.5) * (cutoff_radius / BASIS)
                scaled = (distance - centre) * (1.0 / basis_width)
                radial = jnp.exp(-(scaled * scaled)) * envelope
                for y in range(9):
                    value = radial if y == 0 else harmonics[y] * radial
                    edges[
                        y, k * rows + start : k * rows + start + chunk, column : column + lanes
                    ] = value.astype(edges.dtype)

    edge_half([places[c : c + 1] for c in range(3)], 0)

    for side in range(2):
        if_receives(side, lambda side=side: place_copy(side).wait_recv())
    left = lax.broadcasted_iota(jnp.int32, (1, lanes), 1) < BLOCK
    beside = jnp.where(left, place_in[0, 0:3], place_in[1, 0:3])
    edge_half([beside[c : c + 1] for c in range(3)], lanes)

    for step in range(1, ways):
        weight_copy(step).wait_recv()

    def fold(tile):
        tile = tile + pltpu.roll(tile, width, axis=tile.ndim - 1)
        return tile + pltpu.roll(tile, 2 * width, axis=tile.ndim - 1)

    mine = slot_of == way
    by_step = []
    for step in range(ways):
        held = weight_ref if step == 0 else all_weights.at[step]
        by_step.append([fold(jnp.where(mine, held[n], 0.0)) for n in range(group_paths)])
    spread = []
    for path_number in range(PATHS):
        owner, n = divmod(path_number, group_paths)
        value = by_step[0][n]
        for step in range(1, ways):
            value = jnp.where(lax.rem(way - step + ways, ways) == owner, by_step[step][n], value)
        spread.append(value)

    def tile_weights(g, s, back):
        total = jnp.zeros((BASIS, lanes), jnp.float32)
        for slot in range(SLOTS):
            found = entry(g, s, slot if back else slot ^ s)
            if found is None:
                continue
            sign = found[1] * (parity(g, s) if back else 1.0)
            total = jnp.where(slot_of == slot, sign * spread[found[0]], total)
        return total

    lane_in = lax.broadcasted_iota(jnp.int32, (lanes, lanes), 0)
    lane_out = lax.broadcasted_iota(jnp.int32, (lanes, lanes), 1)
    same_channel = lane_in % width == lane_out % width

    def exchanged(tile, s):
        if s == 0:
            return tile
        matrix = same_channel & ((lane_in // width) == ((lane_out // width) ^ s))
        return jnp.dot(
            tile, matrix.astype(jnp.float32).astype(jnp.bfloat16),
            preferred_element_type=jnp.float32,
        ).astype(jnp.bfloat16)

    def product(source, g, s):
        y = 0 if s == 0 else GROUPS[g][s]
        return jnp.dot(
            edges[y], exchanged(source[g], s), preferred_element_type=jnp.float32
        )

    message = [jnp.zeros((rows, lanes), jnp.float32) for g in range(3)]
    for g, s in TILES:
        if s == 0:
            for side in range(2):
                if_receives(side, lambda side=side, g=g: halo_copy(side, g).wait_recv())
        value = product(table, g, s)
        weights = tile_weights(g, s, False)
        for k in range(BASIS):
            message[g] = message[g] + weights[k : k + 1] * value[k * rows : (k + 1) * rows]

    leading = slot_of == 0
    scalar = fold(jnp.where(leading, message[0] + message[1] + message[2], 0.0))
    sigma = jax.nn.sigmoid(scalar)
    incoming = [cots[g] for g in range(3)]
    coupled = incoming[0] * message[0] + incoming[1] * message[1] + incoming[2] * message[2]
    coupling = fold(jnp.where(leading, 0.0, coupled))
    slope = sigma * (1.0 + scalar * (1.0 - sigma))
    damped = sigma * (1.0 - sigma) * coupling
    for g in range(3):
        gate = jnp.where(leading, incoming[g] * slope + damped, sigma * incoming[g])
        gates[g, 0:rows] = gate.astype(gates.dtype)
        gate_out[0, g] = pick(tail, gate).astype(gate_out.dtype)
        gate_out[1, g] = pick(head, gate).astype(gate_out.dtype)
    for g in range(3):
        for side in range(2):
            if_sends(side, lambda side=side, g=g: gate_copy(side, g).start())

    gradient = [jnp.zeros((rows, lanes), jnp.float32) for g in range(3)]
    parts = [jnp.zeros((BASIS, lanes), jnp.float32) for path_number in range(PATHS)]
    for g, s in TILES:
        if s == 0:
            for side in range(2):
                if_receives(side, lambda side=side, g=g: gate_copy(side, g).wait_recv())
        value = product(gates, g, s)
        weights = tile_weights(g, s, True)
        source = feats[g]
        sums = []
        for k in range(BASIS):
            piece = value[k * rows : (k + 1) * rows]
            gradient[g] = gradient[g] + weights[k : k + 1] * piece
            sums.append(jnp.sum(source * piece, axis=0, keepdims=True))
        summed = jnp.concatenate(sums, axis=0)
        for slot in range(SLOTS):
            found = entry(g, s, slot)
            if found is None:
                continue
            sign = found[1] * parity(g, s)
            parts[found[0]] = parts[found[0]] + jnp.where(slot_of == slot, sign * summed, 0.0)

    totals = [fold(part) for part in parts]
    for t in range(ways):
        tile = jnp.zeros((BASIS, lanes), jnp.float32)
        for n in range(group_paths):
            tile = jnp.where(slot_of == n, totals[t * group_paths + n], tile)
        part_out[t] = tile

    def part_send_step(step, carry):
        other = lax.rem(me + step, count)
        pltpu.make_async_remote_copy(
            src_ref=part_out.at[lax.rem(other, ways)], dst_ref=part_in.at[step - 1],
            send_sem=part_send, recv_sem=part_recv,
            device_id={"box": other // ways, "path": lax.rem(other, ways)}, device_id_type=MESH,
        ).start()
        return carry

    lax.fori_loop(1, count, part_send_step, 0)

    gradient[0] = gradient[0] + jnp.where(leading, gradient[1] + gradient[2], 0.0)
    for g in range(3):
        for t in range(ways):
            grad_out[t, g] = gradient[g][t * share : (t + 1) * share].astype(grad_out.dtype)
        grad_own[g] = gradient[g]

    def grad_copy(step):
        other = lax.rem(way + step, ways)
        return pltpu.make_async_remote_copy(
            src_ref=grad_out.at[other], dst_ref=grad_in.at[step - 1],
            send_sem=grad_send.at[step - 1], recv_sem=grad_recv.at[step - 1],
            device_id={"box": box, "path": other}, device_id_type=MESH,
        )

    for step in range(1, ways):
        grad_copy(step).start()
    own_rows = pl.ds(pl.multiple_of(way * share, share), share)
    for step in range(1, ways):
        grad_copy(step).wait_recv()
    for g in range(3):
        for slot in range(SLOTS):
            component = GROUPS[g][slot]
            if component is None or (g > 0 and slot == 0):
                continue
            total = None
            for step in range(ways):
                owner = lax.rem(way - step + ways, ways)
                held = grad_own[g, own_rows] if step == 0 else grad_in[step - 1, g]
                held = held.astype(jnp.float32)
                shift = lax.rem((owner - slot + ways) * width, lanes)
                moved = jnp.where(slot_of == owner, pltpu.roll(held, shift, axis=1), 0.0)
                total = moved if total is None else total + moved
            grad_ref[component] = total + cot_ref[component, own_rows].astype(jnp.float32)

    whole = pltpu.make_async_copy(part_in, part_in, part_recv)
    whole.wait()
    collected = [part_out[way]] + [None] * (ways - 1)

    def collect(batch, carry):
        return tuple(carry[r] + part_in[batch * ways + r] for r in range(ways))

    empty = tuple(jnp.zeros((BASIS, lanes), jnp.float32) for r in range(ways))
    sums = list(lax.fori_loop(0, boxes - 1, collect, empty))
    for r in range(ways - 1):
        sums[r] = sums[r] + part_in[(boxes - 1) * ways + r]
    collected = [sums[ways - 1] + part_out[way]] + sums[: ways - 1]
    scale = 1.0 / math.sqrt(rows * boxes)
    for n in range(group_paths):
        total = None
        for step in range(ways):
            owner = lax.rem(way - step + ways, ways)
            shift = lax.rem((owner - n + ways) * width, lanes)
            moved = jnp.where(slot_of == owner, pltpu.roll(collected[step], shift, axis=1), 0.0)
            total = moved if total is None else total + moved
        gw_ref[n] = total * scale

    for side in range(2):
        if_sends(side, lambda side=side: place_copy(side).wait_send())
        for g in range(3):
            if_sends(side, lambda side=side, g=g: halo_copy(side, g).wait_send())
            if_sends(side, lambda side=side, g=g: gate_copy(side, g).wait_send())
    for step in range(1, ways):
        weight_copy(step).wait_send()
        grad_copy(step).wait_send()
    pltpu.make_async_copy(part_in, part_in, part_send).wait()


def solution(mesh):
    boxes, ways = mesh.shape["box"], mesh.shape["path"]

    def on_device(features, positions, cotangent, weights, neighbours, send_list):
        rows, components, lanes = features.shape
        share = rows // ways
        reach = rows + 2 * BLOCK
        f32, bf16 = jnp.float32, jnp.bfloat16
        vmem = pl.BlockSpec(memory_space=pltpu.VMEM)
        anywhere = pl.BlockSpec(memory_space=pl.ANY)
        dma = pltpu.SemaphoreType.DMA
        moved, gw = pl.pallas_call(
            functools.partial(kernel, boxes, ways),
            name="layer_back",
            out_shape=(
                jax.ShapeDtypeStruct((components, share, lanes), f32),
                jax.ShapeDtypeStruct((PATHS // ways, BASIS, lanes), f32),
            ),
            in_specs=[anywhere, anywhere, vmem, vmem, pl.BlockSpec(memory_space=pltpu.SMEM)],
            out_specs=(vmem, vmem),
            scratch_shapes=[
                pltpu.VMEM((components, rows, lanes), f32),
                pltpu.VMEM((components, rows, lanes), bf16),
                pltpu.VMEM((components, BASIS * rows, reach), bf16),
                pltpu.VMEM((3, rows, lanes), f32),
                pltpu.VMEM((3, rows, lanes), f32),
                pltpu.VMEM((3, reach, lanes), bf16),
                pltpu.VMEM((3, reach, lanes), bf16),
                pltpu.VMEM((2, 3, BLOCK, lanes), bf16),
                pltpu.VMEM((2, 3, BLOCK, lanes), bf16),
                pltpu.VMEM((2, 8, lanes), f32),
                pltpu.VMEM((2, 8, lanes), f32),
                pltpu.VMEM((ways, PATHS // ways, BASIS, lanes), f32),
                pltpu.VMEM((ways, 3, share, lanes), bf16),
                pltpu.VMEM((ways - 1, 3, share, lanes), bf16),
                pltpu.VMEM((ways, BASIS, lanes), f32),
                pltpu.VMEM((boxes * ways - 1, BASIS, lanes), f32),
                pltpu.VMEM((3, rows, lanes), f32),
                dma((2,)), dma((2,)), dma((2, 3)), dma((2, 3)), dma((2, 3)), dma((2, 3)),
                dma((ways,)), dma((ways,)), dma((ways - 1,)), dma((ways - 1,)), dma, dma,
                dma((2,)),
            ],
            compiler_params=pltpu.CompilerParams(collective_id=0, has_side_effects=True),
        )(
            features.transpose(1, 0, 2), cotangent.transpose(1, 0, 2), positions, weights,
            send_list,
        )
        return moved.transpose(1, 0, 2), gw

    placed = (
        P("box", None, None),
        P(None, "box"),
        P("box", None, None),
        P("path", None, None),
        P("box", None),
        P("box", None),
    )
    return jax.shard_map(
        on_device,
        mesh=mesh,
        in_specs=placed,
        out_specs=(P(("box", "path"), None, None), P("path", None, None)),
        check_vma=False,
    )
```

```python
import functools
import math

import jax
import jax.numpy as jnp
from jax import lax
from jax.experimental import pallas as pl
from jax.experimental.pallas import tpu as pltpu
from jax.sharding import PartitionSpec as P

BASIS = 8
BLOCK = 64
PATHS = 8
SLOTS = 4

cutoff_radius = 5.0
edge_scale = 0.2
basis_width = 0.8
root_three = math.sqrt(3.0)
MESH = pl.DeviceIdType.MESH

GROUPS = ((0, 1, 2, 3), (0, 4, 5, 6), (0, 7, 8, None))
TILES = tuple((g, s) for g in range(3) for s in range(4) if GROUPS[g][s] is not None)
CROSS = {(1, 3): 1.0, (1, 2): -1.0, (2, 1): 1.0, (2, 3): -1.0, (3, 2): 1.0, (3, 1): -1.0}


def entry(g, s, slot):
    if GROUPS[g][slot] is None:
        return None
    if g == 0:
        if s == 0:
            return (0, 1.0) if slot == 0 else (3, 1.0)
        if slot == 0:
            return (2, 1.0)
        if slot == s:
            return (1, 1.0)
        return (6, CROSS[(s, slot)])
    if s == 0:
        return None if slot == 0 else (5, 1.0)
    if slot == 0:
        return (4, 1.0)
    return (7, 1.0) if slot == s else None


def parity(g, s):
    return -1.0 if g == 0 and s > 0 else 1.0


def kernel(
    boxes, ways, feat_hbm, cot_hbm, pos_ref, weight_ref, send_ref, grad_ref, gw_ref,
    feat_ref, cot_ref, edges, feats, cots, table, gates, halo_out, gate_out, place_out, place_in, all_weights,
    grad_out, grad_in, part_out, part_in, grad_own,
    place_send, place_recv, halo_send, halo_recv, gate_send, gate_recv,
    weight_send, weight_recv, grad_send, grad_recv, part_send, part_recv, load_sem,
):
    box = lax.axis_index("box")
    way = lax.axis_index("path")
    count = boxes * ways
    me = box * ways + way
    rows = feat_ref.shape[1]
    lanes = feat_ref.shape[2]
    width = lanes // ways
    share = rows // ways
    group_paths = PATHS // ways

    feat_load = pltpu.make_async_copy(feat_hbm, feat_ref, load_sem.at[0])
    cot_load = pltpu.make_async_copy(cot_hbm, cot_ref, load_sem.at[1])
    feat_load.start()
    cot_load.start()
    barrier = pltpu.get_barrier_semaphore()

    def greet(there, carry):
        for group in range(ways):

            @pl.when((there != box) | (group != way))
            def _():
                pl.semaphore_signal(
                    barrier, inc=1, device_id={"box": there, "path": group},
                    device_id_type=MESH,
                )

        return carry

    lax.fori_loop(0, boxes, greet, 0)

    slot_of = lax.broadcasted_iota(jnp.int32, (1, lanes), 1) // width
    first, last = box == 0, box == boxes - 1

    @pl.when(first)
    def _():
        place_in[0] = jnp.zeros_like(place_in[0])
        table[:, rows : rows + BLOCK] = jnp.zeros((3, BLOCK, lanes), table.dtype)
        gates[:, rows : rows + BLOCK] = jnp.zeros((3, BLOCK, lanes), gates.dtype)

    @pl.when(last)
    def _():
        place_in[1] = jnp.zeros_like(place_in[1])
        table[:, rows + BLOCK :] = jnp.zeros((3, BLOCK, lanes), table.dtype)
        gates[:, rows + BLOCK :] = jnp.zeros((3, BLOCK, lanes), gates.dtype)

    head, tail = send_ref[0, 0], send_ref[0, 1]
    places = pos_ref[...]
    turned = pltpu.roll(places, BLOCK, axis=1)
    place_out[0, 0:3] = jnp.where(tail == 0, places, turned)
    place_out[1, 0:3] = jnp.where(head == 1, places, turned)

    def packed(read, g):
        total = None
        for slot in range(SLOTS):
            component = GROUPS[g][slot]
            if component is None:
                continue
            shift = lax.rem((slot - way + ways) * width, lanes)
            moved = pltpu.roll(read(component), shift, axis=1)
            moved = jnp.where(slot_of == slot, moved, 0.0)
            total = moved if total is None else total + moved
        return total

    def pick(chosen, tile):
        return jnp.where(chosen == 0, tile[:BLOCK], tile[BLOCK:])

    feat_load.wait()
    for g in range(3):
        tile = packed(lambda q: feat_ref[q], g)
        feats[g] = tile
        table[g, 0:rows] = tile.astype(table.dtype)
        halo_out[0, g] = pick(tail, tile).astype(halo_out.dtype)
        halo_out[1, g] = pick(head, tile).astype(halo_out.dtype)

    pl.semaphore_wait(barrier, count - 1)

    def towards(side, source, target, send, recv):
        return pltpu.make_async_remote_copy(
            src_ref=source.at[side], dst_ref=target, send_sem=send.at[side],
            recv_sem=recv.at[side], device_id={"box": box + 1 - 2 * side, "path": way},
            device_id_type=MESH,
        )

    def halo_of(buffer, side):
        return buffer.at[:, pl.ds(rows + side * BLOCK, BLOCK), :]

    def place_copy(side):
        return towards(side, place_out, place_in.at[side], place_send, place_recv)

    def halo_copy(side):
        return towards(side, halo_out, halo_of(table, side), halo_send, halo_recv)

    def gate_copy(side):
        return towards(side, gate_out, halo_of(gates, side), gate_send, gate_recv)

    def if_sends(side, action):
        pl.when(box < boxes - 1 if side == 0 else box > 0)(action)

    def if_receives(side, action):
        pl.when(box > 0 if side == 0 else box < boxes - 1)(action)

    for side in range(2):
        if_sends(side, lambda side=side: place_copy(side).start())
    for side in range(2):
        if_sends(side, lambda side=side: halo_copy(side).start())

    def weight_copy(step):
        return pltpu.make_async_remote_copy(
            src_ref=weight_ref, dst_ref=all_weights.at[step], send_sem=weight_send.at[step],
            recv_sem=weight_recv.at[step],
            device_id={"box": box, "path": lax.rem(way + step, ways)}, device_id_type=MESH,
        )

    for step in range(1, ways):
        weight_copy(step).start()

    cot_load.wait()
    for g in range(3):
        cots[g] = packed(lambda q: cot_ref[q].astype(jnp.float32), g)

    across = [jnp.broadcast_to(places[c : c + 1], (rows, lanes)).T for c in range(3)]

    def edge_half(targets, column):
        chunk = 16
        for start in range(0, rows, chunk):
            offset = [targets[c] - across[c][start : start + chunk] for c in range(3)]
            square = offset[0] * offset[0] + offset[1] * offset[1] + offset[2] * offset[2]
            inside = square > 0.01
            safe = jnp.where(inside, square, 1.0)
            inverse = lax.rsqrt(safe)
            distance = safe * inverse
            east, north, up = [part * inverse for part in offset]
            half = jnp.minimum(distance, cutoff_radius) * (0.5 * math.pi / cutoff_radius)
            z = half * half
            cosine = 1.0 / 479001600.0
            for factor in (3628800.0, 40320.0, 720.0, 24.0, 2.0):
                sign = -1.0 if factor in (3628800.0, 720.0, 2.0) else 1.0
                cosine = cosine * z + sign / factor
            cosine = cosine * z + 1.0
            envelope = jnp.where(
                inside & (distance < cutoff_radius), edge_scale * (cosine * cosine), 0.0
            )
            harmonics = [
                None, east, north, up,
                root_three * east * north,
                root_three * north * up,
                0.5 * (3.0 * up * up - 1.0),
                root_three * east * up,
                0.5 * root_three * (east * east - north * north),
            ]
            for k in range(BASIS):
                centre = (k + 0.5) * (cutoff_radius / BASIS)
                scaled = (distance - centre) * (1.0 / basis_width)
                radial = jnp.exp(-(scaled * scaled)) * envelope
                for y in range(9):
                    value = radial if y == 0 else harmonics[y] * radial
                    edges[
                        y, k * rows + start : k * rows + start + chunk, column : column + lanes
                    ] = value.astype(edges.dtype)

    edge_half([places[c : c + 1] for c in range(3)], 0)

    for side in range(2):
        if_receives(side, lambda side=side: place_copy(side).wait_recv())
    left = lax.broadcasted_iota(jnp.int32, (1, lanes), 1) < BLOCK
    beside = jnp.where(left, place_in[0, 0:3], place_in[1, 0:3])
    edge_half([beside[c : c + 1] for c in range(3)], lanes)

    for step in range(1, ways):
        weight_copy(step).wait_recv()

    def fold(tile):
        tile = tile + pltpu.roll(tile, width, axis=tile.ndim - 1)
        return tile + pltpu.roll(tile, 2 * width, axis=tile.ndim - 1)

    mine = slot_of == way
    by_step = []
    for step in range(ways):
        held = weight_ref if step == 0 else all_weights.at[step]
        by_step.append([fold(jnp.where(mine, held[n], 0.0)) for n in range(group_paths)])
    spread = []
    for path_number in range(PATHS):
        owner, n = divmod(path_number, group_paths)
        value = by_step[0][n]
        for step in range(1, ways):
            value = jnp.where(lax.rem(way - step + ways, ways) == owner, by_step[step][n], value)
        spread.append(value)

    def tile_weights(g, s, back):
        total = jnp.zeros((BASIS, lanes), jnp.float32)
        for slot in range(SLOTS):
            found = entry(g, s, slot if back else slot ^ s)
            if found is None:
                continue
            sign = found[1] * (parity(g, s) if back else 1.0)
            total = jnp.where(slot_of == slot, sign * spread[found[0]], total)
        return total

    lane_in = lax.broadcasted_iota(jnp.int32, (lanes, lanes), 0)
    lane_out = lax.broadcasted_iota(jnp.int32, (lanes, lanes), 1)
    same_channel = lane_in % width == lane_out % width

    def exchanged(tile, s):
        if s == 0:
            return tile
        matrix = same_channel & ((lane_in // width) == ((lane_out // width) ^ s))
        return jnp.dot(
            tile, matrix.astype(jnp.float32).astype(jnp.bfloat16),
            preferred_element_type=jnp.float32,
        ).astype(jnp.bfloat16)

    def product(source, g, s):
        y = 0 if s == 0 else GROUPS[g][s]
        return jnp.dot(
            edges[y], exchanged(source[g], s), preferred_element_type=jnp.float32
        )

    for side in range(2):
        if_receives(side, lambda side=side: halo_copy(side).wait_recv())

    message = [jnp.zeros((rows, lanes), jnp.float32) for g in range(3)]
    for g, s in TILES:
        value = product(table, g, s)
        weights = tile_weights(g, s, False)
        for k in range(BASIS):
            message[g] = message[g] + weights[k : k + 1] * value[k * rows : (k + 1) * rows]

    leading = slot_of == 0
    scalar = fold(jnp.where(leading, message[0] + message[1] + message[2], 0.0))
    sigma = jax.nn.sigmoid(scalar)
    incoming = [cots[g] for g in range(3)]
    coupled = incoming[0] * message[0] + incoming[1] * message[1] + incoming[2] * message[2]
    coupling = fold(jnp.where(leading, 0.0, coupled))
    slope = sigma * (1.0 + scalar * (1.0 - sigma))
    damped = sigma * (1.0 - sigma) * coupling
    for g in range(3):
        gate = jnp.where(leading, incoming[g] * slope + damped, sigma * incoming[g])
        gates[g, 0:rows] = gate.astype(gates.dtype)
        gate_out[0, g] = pick(tail, gate).astype(gate_out.dtype)
        gate_out[1, g] = pick(head, gate).astype(gate_out.dtype)
    for side in range(2):
        if_sends(side, lambda side=side: gate_copy(side).start())
    for side in range(2):
        if_receives(side, lambda side=side: gate_copy(side).wait_recv())

    gradient = [jnp.zeros((rows, lanes), jnp.float32) for g in range(3)]
    parts = [jnp.zeros((BASIS, lanes), jnp.float32) for path_number in range(PATHS)]
    for g, s in TILES:
        value = product(gates, g, s)
        weights = tile_weights(g, s, True)
        source = feats[g]
        sums = []
        for k in range(BASIS):
            piece = value[k * rows : (k + 1) * rows]
            gradient[g] = gradient[g] + weights[k : k + 1] * piece
            sums.append(jnp.sum(source * piece, axis=0, keepdims=True))
        summed = jnp.concatenate(sums, axis=0)
        for slot in range(SLOTS):
            found = entry(g, s, slot)
            if found is None:
                continue
            sign = found[1] * parity(g, s)
            parts[found[0]] = parts[found[0]] + jnp.where(slot_of == slot, sign * summed, 0.0)

    totals = [fold(part) for part in parts]
    for t in range(ways):
        tile = jnp.zeros((BASIS, lanes), jnp.float32)
        for n in range(group_paths):
            tile = jnp.where(slot_of == n, totals[t * group_paths + n], tile)
        part_out[t] = tile.astype(part_out.dtype)

    def part_send_step(step, carry):
        other = lax.rem(me + step, count)
        pltpu.make_async_remote_copy(
            src_ref=part_out.at[lax.rem(other, ways)], dst_ref=part_in.at[step - 1],
            send_sem=part_send, recv_sem=part_recv,
            device_id={"box": other // ways, "path": lax.rem(other, ways)}, device_id_type=MESH,
        ).start()
        return carry

    lax.fori_loop(1, count, part_send_step, 0)

    gradient[0] = gradient[0] + jnp.where(leading, gradient[1] + gradient[2], 0.0)
    for g in range(3):
        for t in range(ways):
            grad_out[t, g] = gradient[g][t * share : (t + 1) * share].astype(grad_out.dtype)
        grad_own[g] = gradient[g]

    def grad_copy(step):
        other = lax.rem(way + step, ways)
        return pltpu.make_async_remote_copy(
            src_ref=grad_out.at[other], dst_ref=grad_in.at[step - 1],
            send_sem=grad_send.at[step - 1], recv_sem=grad_recv.at[step - 1],
            device_id={"box": box, "path": other}, device_id_type=MESH,
        )

    for step in range(1, ways):
        grad_copy(step).start()
    own_rows = pl.ds(pl.multiple_of(way * share, share), share)
    for step in range(1, ways):
        grad_copy(step).wait_recv()
    for g in range(3):
        for slot in range(SLOTS):
            component = GROUPS[g][slot]
            if component is None or (g > 0 and slot == 0):
                continue
            total = None
            for step in range(ways):
                owner = lax.rem(way - step + ways, ways)
                held = grad_own[g, own_rows] if step == 0 else grad_in[step - 1, g]
                held = held.astype(jnp.float32)
                shift = lax.rem((owner - slot + ways) * width, lanes)
                moved = jnp.where(slot_of == owner, pltpu.roll(held, shift, axis=1), 0.0)
                total = moved if total is None else total + moved
            grad_ref[component] = total + cot_ref[component, own_rows].astype(jnp.float32)

    whole = pltpu.make_async_copy(part_in, part_in, part_recv)
    whole.wait()

    def collect(batch, carry):
        return tuple(carry[r] + part_in[batch * ways + r].astype(jnp.float32) for r in range(ways))

    empty = tuple(jnp.zeros((BASIS, lanes), jnp.float32) for r in range(ways))
    sums = list(lax.fori_loop(0, boxes - 1, collect, empty))
    for r in range(ways - 1):
        sums[r] = sums[r] + part_in[(boxes - 1) * ways + r].astype(jnp.float32)
    collected = [sums[ways - 1] + part_out[way].astype(jnp.float32)] + sums[: ways - 1]
    scale = 1.0 / math.sqrt(rows * boxes)
    for n in range(group_paths):
        total = None
        for step in range(ways):
            owner = lax.rem(way - step + ways, ways)
            shift = lax.rem((owner - n + ways) * width, lanes)
            moved = jnp.where(slot_of == owner, pltpu.roll(collected[step], shift, axis=1), 0.0)
            total = moved if total is None else total + moved
        gw_ref[n] = total * scale

    for side in range(2):
        if_sends(side, lambda side=side: place_copy(side).wait_send())
        if_sends(side, lambda side=side: halo_copy(side).wait_send())
        if_sends(side, lambda side=side: gate_copy(side).wait_send())
    for step in range(1, ways):
        weight_copy(step).wait_send()
        grad_copy(step).wait_send()
    pltpu.make_async_copy(part_in, part_in, part_send).wait()


def solution(mesh):
    boxes, ways = mesh.shape["box"], mesh.shape["path"]

    def on_device(features, positions, cotangent, weights, neighbours, send_list):
        rows, components, lanes = features.shape
        share = rows // ways
        reach = rows + 2 * BLOCK
        f32, bf16 = jnp.float32, jnp.bfloat16
        vmem = pl.BlockSpec(memory_space=pltpu.VMEM)
        anywhere = pl.BlockSpec(memory_space=pl.ANY)
        dma = pltpu.SemaphoreType.DMA
        moved, gw = pl.pallas_call(
            functools.partial(kernel, boxes, ways),
            name="layer_back",
            out_shape=(
                jax.ShapeDtypeStruct((components, share, lanes), f32),
                jax.ShapeDtypeStruct((PATHS // ways, BASIS, lanes), f32),
            ),
            in_specs=[anywhere, anywhere, vmem, vmem, pl.BlockSpec(memory_space=pltpu.SMEM)],
            out_specs=(vmem, vmem),
            scratch_shapes=[
                pltpu.VMEM((components, rows, lanes), f32),
                pltpu.VMEM((components, rows, lanes), bf16),
                pltpu.VMEM((components, BASIS * rows, reach), bf16),
                pltpu.VMEM((3, rows, lanes), f32),
                pltpu.VMEM((3, rows, lanes), f32),
                pltpu.VMEM((3, reach, lanes), bf16),
                pltpu.VMEM((3, reach, lanes), bf16),
                pltpu.VMEM((2, 3, BLOCK, lanes), bf16),
                pltpu.VMEM((2, 3, BLOCK, lanes), bf16),
                pltpu.VMEM((2, 8, lanes), f32),
                pltpu.VMEM((2, 8, lanes), f32),
                pltpu.VMEM((ways, PATHS // ways, BASIS, lanes), f32),
                pltpu.VMEM((ways, 3, share, lanes), bf16),
                pltpu.VMEM((ways - 1, 3, share, lanes), bf16),
                pltpu.VMEM((ways, BASIS, lanes), bf16),
                pltpu.VMEM((boxes * ways - 1, BASIS, lanes), bf16),
                pltpu.VMEM((3, rows, lanes), f32),
                dma((2,)), dma((2,)), dma((2,)), dma((2,)), dma((2,)), dma((2,)),
                dma((ways,)), dma((ways,)), dma((ways - 1,)), dma((ways - 1,)), dma, dma,
                dma((2,)),
            ],
            compiler_params=pltpu.CompilerParams(collective_id=0, has_side_effects=True),
        )(
            features.transpose(1, 0, 2), cotangent.transpose(1, 0, 2), positions, weights,
            send_list,
        )
        return moved.transpose(1, 0, 2), gw

    placed = (
        P("box", None, None),
        P(None, "box"),
        P("box", None, None),
        P("path", None, None),
        P("box", None),
        P("box", None),
    )
    return jax.shard_map(
        on_device,
        mesh=mesh,
        in_specs=placed,
        out_specs=(P(("box", "path"), None, None), P("path", None, None)),
        check_vma=False,
    )
```

```python
import functools
import math

import jax
import jax.numpy as jnp
from jax import lax
from jax.experimental import pallas as pl
from jax.experimental.pallas import tpu as pltpu
from jax.sharding import PartitionSpec as P

BASIS = 8
BLOCK = 64
PATHS = 8
SLOTS = 4

cutoff_radius = 5.0
edge_scale = 0.2
basis_width = 0.8
root_three = math.sqrt(3.0)
MESH = pl.DeviceIdType.MESH

GROUPS = ((0, 1, 2, 3), (0, 4, 5, 6), (0, 7, 8, None))
TILES = tuple((g, s) for g in range(3) for s in range(4) if GROUPS[g][s] is not None)
CROSS = {(1, 3): 1.0, (1, 2): -1.0, (2, 1): 1.0, (2, 3): -1.0, (3, 2): 1.0, (3, 1): -1.0}


def entry(g, s, slot):
    if GROUPS[g][slot] is None:
        return None
    if g == 0:
        if s == 0:
            return (0, 1.0) if slot == 0 else (3, 1.0)
        if slot == 0:
            return (2, 1.0)
        if slot == s:
            return (1, 1.0)
        return (6, CROSS[(s, slot)])
    if s == 0:
        return None if slot == 0 else (5, 1.0)
    if slot == 0:
        return (4, 1.0)
    return (7, 1.0) if slot == s else None


def parity(g, s):
    return -1.0 if g == 0 and s > 0 else 1.0


def kernel(
    boxes, ways, feat_hbm, cot_hbm, pos_ref, weight_ref, send_ref, grad_ref, gw_ref,
    feat_ref, cot_ref, edges, feats, cots, table, gates, halo_out, gate_out, place_out, place_in, all_weights,
    grad_out, grad_in, part_out, part_in, grad_own,
    place_send, place_recv, halo_send, halo_recv, gate_send, gate_recv,
    weight_send, weight_recv, grad_send, grad_recv, part_send, part_recv, load_sem,
):
    box = lax.axis_index("box")
    way = lax.axis_index("path")
    count = boxes * ways
    me = box * ways + way
    rows = feat_ref.shape[1]
    lanes = feat_ref.shape[2]
    width = lanes // ways
    share = rows // ways
    group_paths = PATHS // ways

    feat_load = pltpu.make_async_copy(feat_hbm, feat_ref, load_sem.at[0])
    cot_load = pltpu.make_async_copy(cot_hbm, cot_ref, load_sem.at[1])
    feat_load.start()
    cot_load.start()
    barrier = pltpu.get_barrier_semaphore()

    def greet(there, carry):
        for group in range(ways):

            @pl.when((there != box) | (group != way))
            def _():
                pl.semaphore_signal(
                    barrier, inc=1, device_id={"box": there, "path": group},
                    device_id_type=MESH,
                )

        return carry

    lax.fori_loop(0, boxes, greet, 0)

    slot_of = lax.broadcasted_iota(jnp.int32, (1, lanes), 1) // width
    first, last = box == 0, box == boxes - 1

    @pl.when(first)
    def _():
        place_in[0] = jnp.zeros_like(place_in[0])
        table[:, rows : rows + BLOCK] = jnp.zeros((3, BLOCK, lanes), table.dtype)
        gates[:, rows : rows + BLOCK] = jnp.zeros((3, BLOCK, lanes), gates.dtype)

    @pl.when(last)
    def _():
        place_in[1] = jnp.zeros_like(place_in[1])
        table[:, rows + BLOCK :] = jnp.zeros((3, BLOCK, lanes), table.dtype)
        gates[:, rows + BLOCK :] = jnp.zeros((3, BLOCK, lanes), gates.dtype)

    head, tail = send_ref[0, 0], send_ref[0, 1]
    places = pos_ref[...]
    turned = pltpu.roll(places, BLOCK, axis=1)
    place_out[0, 0:3] = jnp.where(tail == 0, places, turned)
    place_out[1, 0:3] = jnp.where(head == 1, places, turned)

    def packed(read, g):
        total = None
        for slot in range(SLOTS):
            component = GROUPS[g][slot]
            if component is None:
                continue
            shift = lax.rem((slot - way + ways) * width, lanes)
            moved = pltpu.roll(read(component), shift, axis=1)
            moved = jnp.where(slot_of == slot, moved, 0.0)
            total = moved if total is None else total + moved
        return total

    def pick(chosen, tile):
        return jnp.where(chosen == 0, tile[:BLOCK], tile[BLOCK:])

    feat_load.wait()
    for g in range(3):
        tile = packed(lambda q: feat_ref[q], g)
        feats[g] = tile
        table[g, 0:rows] = tile.astype(table.dtype)
        halo_out[0, g] = pick(tail, tile).astype(halo_out.dtype)
        halo_out[1, g] = pick(head, tile).astype(halo_out.dtype)

    pl.semaphore_wait(barrier, count - 1)

    def towards(side, source, target, send, recv):
        return pltpu.make_async_remote_copy(
            src_ref=source.at[side], dst_ref=target, send_sem=send.at[side],
            recv_sem=recv.at[side], device_id={"box": box + 1 - 2 * side, "path": way},
            device_id_type=MESH,
        )

    def halo_of(buffer, side):
        return buffer.at[:, pl.ds(rows + side * BLOCK, BLOCK), :]

    def place_copy(side):
        return towards(side, place_out, place_in.at[side], place_send, place_recv)

    def halo_copy(side):
        return towards(side, halo_out, halo_of(table, side), halo_send, halo_recv)

    def gate_copy(side):
        return towards(side, gate_out, halo_of(gates, side), gate_send, gate_recv)

    def if_sends(side, action):
        pl.when(box < boxes - 1 if side == 0 else box > 0)(action)

    def if_receives(side, action):
        pl.when(box > 0 if side == 0 else box < boxes - 1)(action)

    for side in range(2):
        if_sends(side, lambda side=side: place_copy(side).start())
    for side in range(2):
        if_sends(side, lambda side=side: halo_copy(side).start())

    def weight_copy(step):
        return pltpu.make_async_remote_copy(
            src_ref=weight_ref, dst_ref=all_weights.at[step], send_sem=weight_send.at[step],
            recv_sem=weight_recv.at[step],
            device_id={"box": box, "path": lax.rem(way + step, ways)}, device_id_type=MESH,
        )

    for step in range(1, ways):
        weight_copy(step).start()

    cot_load.wait()
    for g in range(3):
        cots[g] = packed(lambda q: cot_ref[q].astype(jnp.float32), g)

    across = [jnp.broadcast_to(places[c : c + 1], (rows, lanes)).T for c in range(3)]

    def edge_half(targets, column):
        chunk = 16
        for start in range(0, rows, chunk):
            offset = [targets[c] - across[c][start : start + chunk] for c in range(3)]
            square = offset[0] * offset[0] + offset[1] * offset[1] + offset[2] * offset[2]
            inside = square > 0.01
            safe = jnp.where(inside, square, 1.0)
            inverse = lax.rsqrt(safe)
            distance = safe * inverse
            east, north, up = [part * inverse for part in offset]
            half = jnp.minimum(distance, cutoff_radius) * (0.5 * math.pi / cutoff_radius)
            z = half * half
            cosine = 1.0 / 479001600.0
            for factor in (3628800.0, 40320.0, 720.0, 24.0, 2.0):
                sign = -1.0 if factor in (3628800.0, 720.0, 2.0) else 1.0
                cosine = cosine * z + sign / factor
            cosine = cosine * z + 1.0
            envelope = jnp.where(
                inside & (distance < cutoff_radius), edge_scale * (cosine * cosine), 0.0
            )
            harmonics = [
                None, east, north, up,
                root_three * east * north,
                root_three * north * up,
                0.5 * (3.0 * up * up - 1.0),
                root_three * east * up,
                0.5 * root_three * (east * east - north * north),
            ]
            for k in range(BASIS):
                centre = (k + 0.5) * (cutoff_radius / BASIS)
                scaled = (distance - centre) * (1.0 / basis_width)
                radial = jnp.exp(-(scaled * scaled)) * envelope
                for y in range(9):
                    value = radial if y == 0 else harmonics[y] * radial
                    edges[
                        y, k * rows + start : k * rows + start + chunk, column : column + lanes
                    ] = value.astype(edges.dtype)

    edge_half([places[c : c + 1] for c in range(3)], 0)

    for side in range(2):
        if_receives(side, lambda side=side: place_copy(side).wait_recv())
    left = lax.broadcasted_iota(jnp.int32, (1, lanes), 1) < BLOCK
    beside = jnp.where(left, place_in[0, 0:3], place_in[1, 0:3])
    edge_half([beside[c : c + 1] for c in range(3)], lanes)

    for step in range(1, ways):
        weight_copy(step).wait_recv()

    def fold(tile):
        tile = tile + pltpu.roll(tile, width, axis=tile.ndim - 1)
        return tile + pltpu.roll(tile, 2 * width, axis=tile.ndim - 1)

    mine = slot_of == way
    by_step = []
    for step in range(ways):
        held = weight_ref if step == 0 else all_weights.at[step]
        by_step.append([fold(jnp.where(mine, held[n], 0.0)) for n in range(group_paths)])
    spread = []
    for path_number in range(PATHS):
        owner, n = divmod(path_number, group_paths)
        value = by_step[0][n]
        for step in range(1, ways):
            value = jnp.where(lax.rem(way - step + ways, ways) == owner, by_step[step][n], value)
        spread.append(value)

    def tile_weights(g, s, back):
        total = jnp.zeros((BASIS, lanes), jnp.float32)
        for slot in range(SLOTS):
            found = entry(g, s, slot if back else slot ^ s)
            if found is None:
                continue
            sign = found[1] * (parity(g, s) if back else 1.0)
            total = jnp.where(slot_of == slot, sign * spread[found[0]], total)
        return total

    lane_in = lax.broadcasted_iota(jnp.int32, (lanes, lanes), 0)
    lane_out = lax.broadcasted_iota(jnp.int32, (lanes, lanes), 1)
    same_channel = lane_in % width == lane_out % width

    def exchanged(tile, s):
        if s == 0:
            return tile
        matrix = same_channel & ((lane_in // width) == ((lane_out // width) ^ s))
        return jnp.dot(
            tile, matrix.astype(jnp.float32).astype(jnp.bfloat16),
            preferred_element_type=jnp.float32,
        ).astype(jnp.bfloat16)

    def product(source, g, s):
        y = 0 if s == 0 else GROUPS[g][s]
        return jnp.dot(
            edges[y], exchanged(source[g], s), preferred_element_type=jnp.float32
        )

    for side in range(2):
        if_receives(side, lambda side=side: halo_copy(side).wait_recv())

    message = [jnp.zeros((rows, lanes), jnp.float32) for g in range(3)]
    for g, s in TILES:
        value = product(table, g, s)
        weights = tile_weights(g, s, False)
        for k in range(BASIS):
            message[g] = message[g] + weights[k : k + 1] * value[k * rows : (k + 1) * rows]

    leading = slot_of == 0
    scalar = fold(jnp.where(leading, message[0] + message[1] + message[2], 0.0))
    sigma = jax.nn.sigmoid(scalar)
    incoming = [cots[g] for g in range(3)]
    coupled = incoming[0] * message[0] + incoming[1] * message[1] + incoming[2] * message[2]
    coupling = fold(jnp.where(leading, 0.0, coupled))
    slope = sigma * (1.0 + scalar * (1.0 - sigma))
    damped = sigma * (1.0 - sigma) * coupling
    for g in range(3):
        gate = jnp.where(leading, incoming[g] * slope + damped, sigma * incoming[g])
        gates[g, 0:rows] = gate.astype(gates.dtype)
        gate_out[0, g] = pick(tail, gate).astype(gate_out.dtype)
        gate_out[1, g] = pick(head, gate).astype(gate_out.dtype)
    for side in range(2):
        if_sends(side, lambda side=side: gate_copy(side).start())
    for side in range(2):
        if_receives(side, lambda side=side: gate_copy(side).wait_recv())

    gradient = [jnp.zeros((rows, lanes), jnp.float32) for g in range(3)]
    parts = [jnp.zeros((BASIS, lanes), jnp.float32) for path_number in range(PATHS)]
    for g, s in TILES:
        value = product(gates, g, s)
        weights = tile_weights(g, s, True)
        source = feats[g]
        sums = []
        for k in range(BASIS):
            piece = value[k * rows : (k + 1) * rows]
            gradient[g] = gradient[g] + weights[k : k + 1] * piece
            sums.append(jnp.sum(source * piece, axis=0, keepdims=True))
        summed = jnp.concatenate(sums, axis=0)
        for slot in range(SLOTS):
            found = entry(g, s, slot)
            if found is None:
                continue
            sign = found[1] * parity(g, s)
            parts[found[0]] = parts[found[0]] + jnp.where(slot_of == slot, sign * summed, 0.0)

    totals = [fold(part) for part in parts]
    for t in range(ways):
        tile = jnp.zeros((BASIS, lanes), jnp.float32)
        for n in range(group_paths):
            tile = jnp.where(slot_of == n, totals[t * group_paths + n], tile)
        part_out[t] = tile.astype(part_out.dtype)

    others = [lax.rem(way + turn, ways) for turn in range(ways)]

    def part_start(ahead, there, turn):
        pltpu.make_async_remote_copy(
            src_ref=part_out.at[others[turn]], dst_ref=part_in.at[ahead * ways + turn - 1],
            send_sem=part_send, recv_sem=part_recv,
            device_id={"box": there, "path": others[turn]}, device_id_type=MESH,
        ).start()

    def part_box(ahead, carry):
        there = lax.rem(box + ahead, boxes)
        for turn in range(ways):
            part_start(ahead, there, turn)
        return carry

    lax.fori_loop(1, boxes, part_box, 0)
    for turn in range(1, ways):
        part_start(0, box, turn)

    gradient[0] = gradient[0] + jnp.where(leading, gradient[1] + gradient[2], 0.0)
    for g in range(3):
        for t in range(ways):
            grad_out[t, g] = gradient[g][t * share : (t + 1) * share].astype(grad_out.dtype)
        grad_own[g] = gradient[g]

    def grad_copy(step):
        other = lax.rem(way + step, ways)
        return pltpu.make_async_remote_copy(
            src_ref=grad_out.at[other], dst_ref=grad_in.at[step - 1],
            send_sem=grad_send.at[step - 1], recv_sem=grad_recv.at[step - 1],
            device_id={"box": box, "path": other}, device_id_type=MESH,
        )

    for step in range(1, ways):
        grad_copy(step).start()
    own_rows = pl.ds(pl.multiple_of(way * share, share), share)
    for step in range(1, ways):
        grad_copy(step).wait_recv()
    for g in range(3):
        for slot in range(SLOTS):
            component = GROUPS[g][slot]
            if component is None or (g > 0 and slot == 0):
                continue
            total = None
            for step in range(ways):
                owner = lax.rem(way - step + ways, ways)
                held = grad_own[g, own_rows] if step == 0 else grad_in[step - 1, g]
                held = held.astype(jnp.float32)
                shift = lax.rem((owner - slot + ways) * width, lanes)
                moved = jnp.where(slot_of == owner, pltpu.roll(held, shift, axis=1), 0.0)
                total = moved if total is None else total + moved
            grad_ref[component] = total + cot_ref[component, own_rows].astype(jnp.float32)

    whole = pltpu.make_async_copy(part_in, part_in, part_recv)
    whole.wait()

    def collect(batch, carry):
        return tuple(carry[r] + part_in[batch * ways + r].astype(jnp.float32) for r in range(ways))

    empty = tuple(jnp.zeros((BASIS, lanes), jnp.float32) for r in range(ways))
    sums = list(lax.fori_loop(0, boxes - 1, collect, empty))
    for r in range(ways - 1):
        sums[r] = sums[r] + part_in[(boxes - 1) * ways + r].astype(jnp.float32)
    collected = [sums[ways - 1] + part_out[way].astype(jnp.float32)] + sums[: ways - 1]
    scale = 1.0 / math.sqrt(rows * boxes)
    for n in range(group_paths):
        total = None
        for step in range(ways):
            owner = lax.rem(way - step + ways, ways)
            shift = lax.rem((owner - n + ways) * width, lanes)
            moved = jnp.where(slot_of == owner, pltpu.roll(collected[step], shift, axis=1), 0.0)
            total = moved if total is None else total + moved
        gw_ref[n] = total * scale

    for side in range(2):
        if_sends(side, lambda side=side: place_copy(side).wait_send())
        if_sends(side, lambda side=side: halo_copy(side).wait_send())
        if_sends(side, lambda side=side: gate_copy(side).wait_send())
    for step in range(1, ways):
        weight_copy(step).wait_send()
        grad_copy(step).wait_send()
    pltpu.make_async_copy(part_in, part_in, part_send).wait()


def solution(mesh):
    boxes, ways = mesh.shape["box"], mesh.shape["path"]

    def on_device(features, positions, cotangent, weights, neighbours, send_list):
        rows, components, lanes = features.shape
        share = rows // ways
        reach = rows + 2 * BLOCK
        f32, bf16 = jnp.float32, jnp.bfloat16
        vmem = pl.BlockSpec(memory_space=pltpu.VMEM)
        anywhere = pl.BlockSpec(memory_space=pl.ANY)
        dma = pltpu.SemaphoreType.DMA
        moved, gw = pl.pallas_call(
            functools.partial(kernel, boxes, ways),
            name="layer_back",
            out_shape=(
                jax.ShapeDtypeStruct((components, share, lanes), f32),
                jax.ShapeDtypeStruct((PATHS // ways, BASIS, lanes), f32),
            ),
            in_specs=[anywhere, anywhere, vmem, vmem, pl.BlockSpec(memory_space=pltpu.SMEM)],
            out_specs=(vmem, vmem),
            scratch_shapes=[
                pltpu.VMEM((components, rows, lanes), f32),
                pltpu.VMEM((components, rows, lanes), bf16),
                pltpu.VMEM((components, BASIS * rows, reach), bf16),
                pltpu.VMEM((3, rows, lanes), f32),
                pltpu.VMEM((3, rows, lanes), f32),
                pltpu.VMEM((3, reach, lanes), bf16),
                pltpu.VMEM((3, reach, lanes), bf16),
                pltpu.VMEM((2, 3, BLOCK, lanes), bf16),
                pltpu.VMEM((2, 3, BLOCK, lanes), bf16),
                pltpu.VMEM((2, 8, lanes), f32),
                pltpu.VMEM((2, 8, lanes), f32),
                pltpu.VMEM((ways, PATHS // ways, BASIS, lanes), f32),
                pltpu.VMEM((ways, 3, share, lanes), bf16),
                pltpu.VMEM((ways - 1, 3, share, lanes), bf16),
                pltpu.VMEM((ways, BASIS, lanes), bf16),
                pltpu.VMEM((boxes * ways - 1, BASIS, lanes), bf16),
                pltpu.VMEM((3, rows, lanes), f32),
                dma((2,)), dma((2,)), dma((2,)), dma((2,)), dma((2,)), dma((2,)),
                dma((ways,)), dma((ways,)), dma((ways - 1,)), dma((ways - 1,)), dma, dma,
                dma((2,)),
            ],
            compiler_params=pltpu.CompilerParams(collective_id=0, has_side_effects=True),
        )(
            features.transpose(1, 0, 2), cotangent.transpose(1, 0, 2), positions, weights,
            send_list,
        )
        return moved.transpose(1, 0, 2), gw

    placed = (
        P("box", None, None),
        P(None, "box"),
        P("box", None, None),
        P("path", None, None),
        P("box", None),
        P("box", None),
    )
    return jax.shard_map(
        on_device,
        mesh=mesh,
        in_specs=placed,
        out_specs=(P(("box", "path"), None, None), P("path", None, None)),
        check_vma=False,
    )
```
